128 devices in a mesh: shot: 4 (over z_hi, core), gx: 16 (over x, y), gy: 2 (over z_lo).
Axes of the slice: x: 4, y: 4, z: 4 (z_hi: 2, z_lo: 2; z = z_hi * 2 + z_lo), core: 2. Of those that a mesh axis runs over, the one named last changes fastest.
Arguments:
- wave_now: float32 [4, 4, 512, 64, 128], P('shot', None, 'gx', 'gy'), may hold values from -6 to 6
- wave_prev: float32 [4, 4, 512, 64, 128], P('shot', None, 'gx', 'gy'), may hold values from -6 to 6
- vel_coef: float32 [512, 64, 128], P('gx', 'gy'), may hold values from 0.08 to 0.18
- epsilon: float32 [512, 64, 128], P('gx', 'gy'), may hold values from 0.15 to 0.35
- delta: float32 [512, 64, 128], P('gx', 'gy'), may hold values from 0 to 0.15
- tilt: int32 [512, 64, 128], P('gx', 'gy'), may hold values from 0 to 60
- azimuth: int32 [512, 64, 128], P('gx', 'gy'), may hold values from 0 to 359
- aperture: int32 [4, 16, 2], P('shot', 'gx', 'gy'), may hold values 0 or 1
Outputs:
- wave_final: float32 [4, 4, 512, 64, 128], P('shot', None, 'gx', 'gy')
- image: float32 [512, 64, 128], P('gx', 'gy')
The draws below stay inside these ranges and needn't reach their ends.
All inputs are finite; a program needn't handle non-finite values. No bound on the sum of `aperture` on one device may be relied on, other than what follows from the above.
Results may differ from the reference program's by a relative error of at most 0.00002.
Values sent between devices are 32-bit elements; how exact they have to be, the bound alone decides.
A program may use at most 128 MiB of HBM per device.

```python
import math
import jax
import jax.numpy as jnp

CX = 32
CY = 32
ITERS = 4
FIELDS = 4
SHOTS = 4
NX = 512
NY = 64
NZ = 128
TILES_X = 16
TILES_Y = 2


def place_ends(entries, rng, least, top_value):
    longest = entries.shape.index(max(entries.shape))
    spots = []
    for shift in (0, 1):
        where = [jax.random.randint(jax.random.fold_in(rng, axis), (), 0, length) for axis, length in enumerate(entries.shape)]
        where[longest] = (where[longest] + shift) % entries.shape[longest]
        spots.append(tuple(where))
    return entries.at[spots[0]].set(least).at[spots[1]].set(top_value)


def shard_levels(stream_key, shape, cuts, low, top_value):
    factor_of = 1.0
    for dim, blocks in cuts:
        draws = jax.random.uniform(jax.random.fold_in(jax.random.fold_in(stream_key, 6), dim), (blocks,), jnp.float32, low / len(cuts), top_value / len(cuts))
        factor_of = factor_of * jnp.repeat(jnp.exp(draws), shape[dim] // blocks).reshape((-1,) + (1,) * (len(shape) - 1 - dim))
    return factor_of


def centred(rng, shape, width, limit, split=(), kind=jnp.bfloat16):
    result = width * jax.random.normal(rng, shape, jnp.float32)
    if split:
        result = result * shard_levels(rng, shape, split, -0.22, 0.18)
    return jnp.clip(result, -limit, limit).astype(kind)


def setup_inputs(seed: int = 0) -> dict:
    streams_of = jax.random.split(jax.random.key(seed), 9)
    return {
        "wave_now": centred(streams_of[0], (SHOTS, FIELDS, NX, NY, NZ), 1.0, 6.0, ((0, 4), (2, 16), (3, 2)), jnp.float32),
        "wave_prev": centred(streams_of[1], (SHOTS, FIELDS, NX, NY, NZ), 1.0, 6.0, ((0, 4), (2, 16), (3, 2)), jnp.float32),
        "vel_coef": jnp.clip(jnp.exp(math.log(0.18) - 0.81093028 * jax.random.uniform(streams_of[2], (NX, NY, NZ), jnp.float32) ** shard_levels(streams_of[2], (NX, NY, NZ), ((0, 16), (1, 2)), -0.2, 0.2)), 0.08, 0.18),
        "epsilon": jnp.clip(0.15 + 0.19999999 * jax.random.uniform(streams_of[3], (NX, NY, NZ), jnp.float32) ** shard_levels(streams_of[3], (NX, NY, NZ), ((0, 16), (1, 2)), -0.2, 0.2), 0.15, 0.35),
        "delta": jnp.clip(0.15 * jax.random.uniform(streams_of[4], (NX, NY, NZ), jnp.float32) ** shard_levels(streams_of[4], (NX, NY, NZ), ((0, 16), (1, 2)), -0.2, 0.2), 0.0, 0.15),
        "tilt": place_ends(jax.random.randint(streams_of[5], (NX, NY, NZ), 0, 61), jax.random.fold_in(streams_of[5], 1), 0, 60).astype(jnp.int32),
        "azimuth": place_ends(jax.random.randint(streams_of[6], (NX, NY, NZ), 0, 360), jax.random.fold_in(streams_of[6], 1), 0, 359).astype(jnp.int32),
        "aperture": place_ends((jax.random.randint(streams_of[7], (SHOTS, TILES_X, TILES_Y), 0, 4) < 3).astype(jnp.int32), jax.random.fold_in(streams_of[7], 1), 0, 1),
    }


def model_terms(vel_coef, epsilon, delta, tilt, azimuth):
    theta = tilt.astype(jnp.float32) * (math.pi / 180.0)
    phi = azimuth.astype(jnp.float32) * (math.pi / 180.0)
    normal_x = jnp.sin(theta) * jnp.cos(phi)
    normal_y = jnp.sin(theta) * jnp.sin(phi)
    normal_z = jnp.cos(theta)
    gain = 1.0 + 2.0 * epsilon
    root = jnp.sqrt(1.0 + 2.0 * delta)
    return jnp.stack([normal_x, normal_y, normal_z, vel_coef, gain, root], axis=0)

def advance(padded, previous, coef):
    width_x = padded.shape[-3] - 2
    width_y = padded.shape[-2] - 2
    width_z = padded.shape[-1] - 2

    def shifted(off_x, off_y, off_z):
        return padded[..., 1 + off_x:1 + off_x + width_x, 1 + off_y:1 + off_y + width_y, 1 + off_z:1 + off_z + width_z]
    centre = shifted(0, 0, 0)
    second_x = shifted(1, 0, 0) + shifted(-1, 0, 0) - 2.0 * centre
    second_y = shifted(0, 1, 0) + shifted(0, -1, 0) - 2.0 * centre
    second_z = shifted(0, 0, 1) + shifted(0, 0, -1) - 2.0 * centre
    mixed_xy = 0.25 * (shifted(1, 1, 0) - shifted(1, -1, 0) - shifted(-1, 1, 0) + shifted(-1, -1, 0))
    mixed_xz = 0.25 * (shifted(1, 0, 1) - shifted(1, 0, -1) - shifted(-1, 0, 1) + shifted(-1, 0, -1))
    mixed_yz = 0.25 * (shifted(0, 1, 1) - shifted(0, 1, -1) - shifted(0, -1, 1) + shifted(0, -1, -1))
    normal_x, normal_y, normal_z = (coef[0], coef[1], coef[2])
    speed, gain, root = (coef[3], coef[4], coef[5])
    along = normal_x * normal_x * second_x + normal_y * normal_y * second_y + normal_z * normal_z * second_z + 2.0 * (normal_x * normal_y * mixed_xy + normal_x * normal_z * mixed_xz + normal_y * normal_z * mixed_yz)
    across = second_x + second_y + second_z - along
    pressure = centre[:, 0::2]
    auxiliary = centre[:, 1::2]
    rhs_p = gain * across[:, 0::2] + root * along[:, 1::2]
    rhs_q = root * across[:, 0::2] + along[:, 1::2]
    next_p = 2.0 * pressure - previous[:, 0::2] + speed * rhs_p
    next_q = 2.0 * auxiliary - previous[:, 1::2] + speed * rhs_q
    return jnp.stack([next_p, next_q], axis=2).reshape(centre.shape)

def reference(wave_now, wave_prev, vel_coef, epsilon, delta, tilt, azimuth, aperture):
    coef = model_terms(vel_coef, epsilon, delta, tilt, azimuth)
    finals = []
    image = jnp.zeros(vel_coef.shape, jnp.float32)
    for shot_index in range(SHOTS):
        current = wave_now[shot_index:shot_index + 1]
        previous = wave_prev[shot_index:shot_index + 1]
        correlation = jnp.zeros(vel_coef.shape, jnp.float32)
        for step in range(ITERS):
            padded = jnp.pad(current, ((0, 0), (0, 0), (1, 1), (1, 1), (1, 1)))
            fresh = advance(padded, previous, coef)
            correlation = correlation + fresh[0, 0] * fresh[0, 2]
            previous, current = (current, fresh)
        finals.append(current)
        covered = jnp.repeat(jnp.repeat(aperture[shot_index].astype(jnp.float32), CX, axis=0), CY, axis=1)
        image = image + covered[:, :, None] * correlation
    return (jnp.concatenate(finals, axis=0), image / ITERS)
```

```python
import functools
import math

import jax
import jax.numpy as jnp
from jax import lax
from jax.experimental import pallas as pl
from jax.experimental.pallas import tpu as pltpu
from jax.sharding import PartitionSpec as P

ITERS = 4
F = 4
PAD = 8
MESH = pl.DeviceIdType.MESH
NK = 12
AXX, AYY, BXY, AP, AM, BP, BM, CP, CM, CG, CR, CV = range(NK)


def sin_poly(x, x2):
    return x * (1.0 + x2 * (-1.0 / 6 + x2 * (1.0 / 120 + x2 * (-1.0 / 5040 + x2 * (1.0 / 362880 - x2 * (1.0 / 39916800))))))


def cos_poly(x2):
    return 1.0 + x2 * (-0.5 + x2 * (1.0 / 24 + x2 * (-1.0 / 720 + x2 * (1.0 / 40320 + x2 * (-1.0 / 3628800 + x2 * (1.0 / 479001600))))))


def normals(tilt, azimuth):
    theta = tilt.astype(jnp.float32) * (math.pi / 180.0)
    t2 = theta * theta
    sin_t, cos_t = sin_poly(theta, t2), cos_poly(t2)
    b1, b2, b3, b4 = (azimuth >= edge for edge in (45, 135, 225, 315))
    zero, step = jnp.zeros_like(azimuth), jnp.full_like(azimuth, 90)
    base = jnp.where(b1, step, zero) + jnp.where(b2, step, zero) + jnp.where(b3, step, zero) + jnp.where(b4, step, zero)
    rest = (azimuth - base).astype(jnp.float32) * (math.pi / 180.0)
    r2 = rest * rest
    s, c = sin_poly(rest, r2), cos_poly(r2)
    odd = (base == 90) | (base == 270)
    sin_m = jnp.where(odd, c, s)
    cos_m = jnp.where(odd, s, c)
    sin_neg = (base == 180) | (base == 270)
    cos_neg = (base == 90) | (base == 180)
    sin_p = jnp.where(sin_neg, -sin_m, sin_m)
    cos_p = jnp.where(cos_neg, -cos_m, cos_m)
    return sin_t * cos_p, sin_t * sin_p, cos_t


def kernel(sizes, now, prev, vel, eps, dlt, tilt, azim, aper, wave_out, img_out,
           U, M, A, K, corr, P_, Q, PC, QC, R1, R2, IMG, local, ssem, rsem, isem, osem):
    ngx, X, Y, Z = sizes
    T = Y // 8
    shot, gx, gy = lax.axis_index("shot"), lax.axis_index("gx"), lax.axis_index("gy")
    has_l, has_r = gx > 0, gx < ngx - 1
    core = lax.rem(shot, 2)
    core_pair = shot + 1 - 2 * core
    z_pair = lax.rem(shot + 2, 4)
    left, right, other = gx - 1, gx + 1, 1 - gy
    dev_l, dev_r, dev_y = (shot, left, gy), (shot, right, gy), (shot, gx, other)
    dev_dl, dev_dr = (shot, left, other), (shot, right, other)
    dev_c, dev_z = (core_pair, gx, gy), (z_pair, gx, gy)
    y_send = PAD + (Y - 1) * (1 - gy)
    y_recv = PAD - 1 + (Y + 1) * (1 - gy)

    loads = [pltpu.make_async_copy(now.at[0], U.at[0, :, pl.ds(1, X), pl.ds(PAD, Y), :], local.at[0])]
    for i, ref in enumerate((tilt, azim)):
        loads.append(pltpu.make_async_copy(ref, A.at[i], local.at[1 + i]))
    for i, ref in enumerate((vel, eps, dlt)):
        loads.append(pltpu.make_async_copy(ref, M.at[i], local.at[3 + i]))
    loads.append(pltpu.make_async_copy(prev.at[0], U.at[1, :, pl.ds(1, X), pl.ds(PAD, Y), :], local.at[6]))
    for copy in loads:
        copy.start()

    barrier = pltpu.get_barrier_semaphore()

    def hello(dev):
        pl.semaphore_signal(barrier, inc=1, device_id=dev, device_id_type=MESH)

    for dev in (dev_y, dev_c, dev_z):
        hello(dev)

    @pl.when(has_l)
    def _():
        hello(dev_l)
        hello(dev_dl)

    @pl.when(has_r)
    def _():
        hello(dev_r)
        hello(dev_dr)

    zero_tile = jnp.zeros((8, Z), jnp.float32)

    def zero_rows(x, c):
        for par in range(2):
            for f in range(F):
                U[par, f, x, pl.ds(0, 8), :] = zero_tile
                U[par, f, x, pl.ds(PAD + Y, 8), :] = zero_tile
        return c

    lax.fori_loop(0, X + 2, zero_rows, 0)

    def zero_plane(x):
        for par in range(2):
            for f in range(F):
                for j in range(T):
                    U[par, f, x, pl.ds(PAD + 8 * j, 8), :] = zero_tile

    @pl.when(jnp.logical_not(has_l))
    def _():
        zero_plane(0)

    @pl.when(jnp.logical_not(has_r))
    def _():
        zero_plane(X + 1)

    pl.semaphore_wait(barrier, 3 + 2 * has_l.astype(jnp.int32) + 2 * has_r.astype(jnp.int32))

    def halo(t, d):
        par = t % 2

        def plane(x):
            if t == 0:
                return now.at[0, :, x - 1]
            return U.at[par, :, x, pl.ds(PAD, Y), :]

        def make(d, src, dst, dev):
            return pltpu.make_async_remote_copy(
                src_ref=src, dst_ref=dst, send_sem=ssem.at[t, d], recv_sem=rsem.at[t, d],
                device_id=dev, device_id_type=MESH)

        if d == 0:
            return make(0, plane(1), U.at[par, :, X + 1, pl.ds(PAD, Y), :], dev_l)
        if d == 1:
            return make(1, plane(X), U.at[par, :, 0, pl.ds(PAD, Y), :], dev_r)
        if d == 2:
            return make(2, P_.at[t], Q.at[t], dev_y)
        if d == 3:
            return make(3, PC.at[t, 0], QC.at[t, 1], dev_dl)
        return make(4, PC.at[t, 1], QC.at[t, 0], dev_dr)

    def send_x(t):
        @pl.when(has_l)
        def _():
            halo(t, 0).start()

        @pl.when(has_r)
        def _():
            halo(t, 1).start()

    def send_y(t):
        par = t % 2
        for f in range(F):
            P_[t, f] = U[par, f, pl.ds(1, X), y_send, :]
            PC[t, 0, pl.ds(f, 1), :] = U[par, f, 1, pl.ds(y_send, 1), :]
            PC[t, 1, pl.ds(f, 1), :] = U[par, f, X, pl.ds(y_send, 1), :]
        halo(t, 2).start()

        @pl.when(has_l)
        def _():
            halo(t, 3).start()

        @pl.when(has_r)
        def _():
            halo(t, 4).start()

    def receive(t):
        par = t % 2
        halo(t, 2).wait_recv()
        for f in range(F):
            U[par, f, pl.ds(1, X), y_recv, :] = Q[t, f]

        @pl.when(has_r)
        def _():
            halo(t, 0).wait_recv()
            halo(t, 3).wait_recv()
            for f in range(F):
                U[par, f, X + 1, pl.ds(y_recv, 1), :] = QC[t, 1, pl.ds(f, 1), :]

        @pl.when(has_l)
        def _():
            halo(t, 1).wait_recv()
            halo(t, 4).wait_recv()
            for f in range(F):
                U[par, f, 0, pl.ds(y_recv, 1), :] = QC[t, 0, pl.ds(f, 1), :]

    def sent(t):
        halo(t, 2).wait_send()

        @pl.when(has_l)
        def _():
            halo(t, 0).wait_send()
            halo(t, 3).wait_send()

        @pl.when(has_r)
        def _():
            halo(t, 1).wait_send()
            halo(t, 4).wait_send()

    send_x(0)
    loads[0].wait()
    send_y(0)

    lane = lax.broadcasted_iota(jnp.int32, (8, Z), 1)
    mask_p = jnp.where(lane == 0, 0.0, 1.0)
    mask_m = jnp.where(lane == Z - 1, 0.0, 1.0)
    for i in range(1, 6):
        loads[i].wait()

    def model(x, c):
        for j in range(T):
            rows = pl.ds(8 * j, 8)
            n_x, n_y, n_z = normals(A[0, x, rows, :], A[1, x, rows, :])
            v = M[0, x, rows, :]
            gain = 1.0 + 2.0 * M[1, x, rows, :]
            root = jnp.sqrt(1.0 + 2.0 * M[2, x, rows, :])
            half = 0.5 * n_z
            zz, xz, yz = n_z * n_z, half * n_x, half * n_y
            K[AXX, x, rows, :] = n_x * n_x
            K[AYY, x, rows, :] = n_y * n_y
            K[BXY, x, rows, :] = 0.5 * n_x * n_y
            for value, plus, minus in ((zz, AP, AM), (xz, BP, BM), (yz, CP, CM)):
                K[plus, x, rows, :] = pltpu.roll(value, 1, 1) * mask_p
                K[minus, x, rows, :] = pltpu.roll(value, Z - 1, 1) * mask_m
            K[CG, x, rows, :] = v * gain
            K[CR, x, rows, :] = v * root
            K[CV, x, rows, :] = v
        return c

    lax.fori_loop(0, X, model, 0)
    loads[6].wait()
    covered = aper[0, 0, 0].astype(jnp.float32) * (1.0 / ITERS)

    def segment(t, row, first, count, unroll):
        a, b = t % 2, 1 - t % 2
        row = pl.multiple_of(row, 8)
        yrow = pl.multiple_of(row - PAD, 8)

        def plane(f, x):
            mid = U[a, f, x, pl.ds(row, 8), :]
            up, down = U[a, f, x, pl.ds(row + 1, 8), :], U[a, f, x, pl.ds(row - 1, 8), :]
            return mid, up - down, up + down

        def body(x, carry):
            rows = pl.ds(yrow, 8)
            k = [K[i, x - 1, rows, :] for i in range(NK)]
            cxx, cyy = 1.0 - k[AXX], 1.0 - k[AYY]
            cap, cam = mask_p - k[AP], mask_m - k[AM]
            ahead, fresh, op = [], [], []
            for f in range(F):
                f0, e0, f1, e1, ys = carry[f]
                f2, e2, ys2 = plane(f, x + 1)
                ahead.append((f1, e1, f2, e2, ys2))
                xs, dx, exy = f2 + f0, f2 - f0, e2 - e0
                tp = k[BP] * dx + k[CP] * e1
                tm = k[BM] * dx + k[CM] * e1
                mix = k[BXY] * exy
                if f % 2 == 0:
                    sp, sm = cap * f1 - tp, cam * f1 + tm
                    side = cxx * xs + cyy * ys - mix
                else:
                    sp, sm = k[AP] * f1 + tp, k[AM] * f1 - tm
                    side = k[AXX] * xs + k[AYY] * ys + mix
                op.append(side + (pltpu.roll(sp, Z - 1, 1) + pltpu.roll(sm, 1, 1)))
            for pair in range(F // 2):
                p, q = carry[2 * pair][2], carry[2 * pair + 1][2]
                p2, q2 = p + p, q + q
                across = op[2 * pair] - (p2 + p2)
                along = op[2 * pair + 1] - q2
                p_old = U[b, 2 * pair, x, pl.ds(row, 8), :]
                q_old = U[b, 2 * pair + 1, x, pl.ds(row, 8), :]
                p_new = (p2 - p_old) + (k[CG] * across + k[CR] * along)
                q_new = (q2 - q_old) + (k[CR] * across + k[CV] * along)
                U[b, 2 * pair, x, pl.ds(row, 8), :] = p_new
                U[b, 2 * pair + 1, x, pl.ds(row, 8), :] = q_new
                fresh.append(p_new)
            prod = fresh[0] * fresh[1]
            if t > 0:
                prod = prod + corr[x - 1, rows, :]
            if t == ITERS - 1:
                prod = prod * covered
            corr[x - 1, rows, :] = prod
            return tuple(ahead)

        def start(f):
            f0, e0, _ = plane(f, first - 1)
            return (f0, e0) + plane(f, first)

        carry = tuple(start(f) for f in range(F))

        def several(i, carry):
            for u in range(unroll):
                carry = body(first + i * unroll + u, carry)
            return carry

        if count == unroll:
            several(0, carry)
        else:
            lax.fori_loop(0, count // unroll, several, carry)

    edge_row = PAD + (Y - 8) * (1 - gy)
    inner_row = PAD + 8 * gy
    for t in range(ITERS):
        receive(t)
        if t > 0:
            sent(t - 1)
        segment(t, edge_row, 1, X, 2)

        def ends(k, c, t=t):
            segment(t, inner_row + 8 * k, 1, 1, 1)
            segment(t, inner_row + 8 * k, X, 1, 1)
            return c

        lax.fori_loop(0, T - 1, ends, 0)
        if t < ITERS - 1:
            send_x(t + 1)
            send_y(t + 1)

        def inner(k, c, t=t):
            segment(t, inner_row + 8 * k, 2, X - 2, 2)
            return c

        lax.fori_loop(0, T - 1, inner, 0)
    sent(ITERS - 1)

    last = ITERS % 2
    store = pltpu.make_async_copy(U.at[last, :, pl.ds(1, X), pl.ds(PAD, Y), :], wave_out.at[0], osem.at[0])
    store.start()

    H = X // 2
    mine, theirs = pl.ds(core * H, H), pl.ds((1 - core) * H, H)

    def image_copy(i, src, dst, dev):
        return pltpu.make_async_remote_copy(
            src_ref=src, dst_ref=dst, send_sem=isem.at[0, i], recv_sem=isem.at[1, i],
            device_id=dev, device_id_type=MESH)

    first = image_copy(0, corr.at[theirs], R1, dev_c)
    first.start()
    first.wait()

    def add1(x, c):
        for j in range(T):
            rows = pl.ds(8 * j, 8)
            R1[x, rows, :] = R1[x, rows, :] + corr[core * H + x, rows, :]
        return c

    lax.fori_loop(0, H, add1, 0)
    second = image_copy(1, R1, R2, dev_z)
    second.start()
    second.wait()

    def add2(x, c):
        for j in range(T):
            rows = pl.ds(8 * j, 8)
            IMG[core * H + x, rows, :] = R1[x, rows, :] + R2[x, rows, :]
        return c

    lax.fori_loop(0, H, add2, 0)
    third = image_copy(2, IMG.at[mine], IMG.at[mine], dev_c)
    third.start()
    third.wait()
    out = pltpu.make_async_copy(IMG, img_out, osem.at[1])
    out.start()
    out.wait()
    store.wait()


def solution(mesh):
    ngx = mesh.shape["gx"]

    def local(now, prev, vel, eps, dlt, tilt, azim, aper):
        X, Y, Z = vel.shape
        any_, vm = pl.BlockSpec(memory_space=pl.ANY), pltpu.VMEM
        f32 = jnp.float32
        return pl.pallas_call(
            functools.partial(kernel, (ngx, X, Y, Z)),
            out_shape=(jax.ShapeDtypeStruct(now.shape, f32), jax.ShapeDtypeStruct(vel.shape, f32)),
            in_specs=[any_] * 7 + [pl.BlockSpec(memory_space=pltpu.SMEM)],
            out_specs=(any_, any_),
            scratch_shapes=[
                vm((2, F, X + 2, Y + 2 * PAD, Z), f32),
                vm((3, X, Y, Z), f32),
                vm((2, X, Y, Z), jnp.int32),
                vm((NK, X, Y, Z), f32),
                vm((X, Y, Z), f32),
                vm((ITERS, F, X, Z), f32),
                vm((ITERS, F, X, Z), f32),
                vm((ITERS, 2, F, Z), f32),
                vm((ITERS, 2, F, Z), f32),
                vm((X // 2, Y, Z), f32),
                vm((X // 2, Y, Z), f32),
                vm((X, Y, Z), f32),
                pltpu.SemaphoreType.DMA((7,)),
                pltpu.SemaphoreType.DMA((ITERS, 5)),
                pltpu.SemaphoreType.DMA((ITERS, 5)),
                pltpu.SemaphoreType.DMA((2, 3)),
                pltpu.SemaphoreType.DMA((2,)),
            ],
            compiler_params=pltpu.CompilerParams(
                collective_id=0, has_side_effects=True, vmem_limit_bytes=56 * 1024 * 1024),
        )(now, prev, vel, eps, dlt, tilt, azim, aper)

    return jax.shard_map(
        local,
        mesh=mesh,
        in_specs=(
            P("shot", None, "gx", "gy", None),
            P("shot", None, "gx", "gy", None),
            P("gx", "gy", None),
            P("gx", "gy", None),
            P("gx", "gy", None),
            P("gx", "gy", None),
            P("gx", "gy", None),
            P("shot", "gx", "gy"),
        ),
        out_specs=(P("shot", None, "gx", "gy", None), P("gx", "gy", None)),
        check_vma=False,
    )
```

```python
import functools
import math

import jax
import jax.numpy as jnp
from jax import lax
from jax.experimental import pallas as pl
from jax.experimental.pallas import tpu as pltpu
from jax.sharding import PartitionSpec as P

ITERS = 4
F = 4
PAD = 8
MESH = pl.DeviceIdType.MESH
NK = 12
AXX, AYY, BXY, AP, AM, BP, BM, CP, CM, CG, CR, CV = range(NK)


def sin_poly(x, x2):
    return x * (1.0 + x2 * (-1.0 / 6 + x2 * (1.0 / 120 + x2 * (-1.0 / 5040 + x2 * (1.0 / 362880 - x2 * (1.0 / 39916800))))))


def cos_poly(x2):
    return 1.0 + x2 * (-0.5 + x2 * (1.0 / 24 + x2 * (-1.0 / 720 + x2 * (1.0 / 40320 + x2 * (-1.0 / 3628800 + x2 * (1.0 / 479001600))))))


def normals(tilt, azimuth):
    theta = tilt.astype(jnp.float32) * (math.pi / 180.0)
    t2 = theta * theta
    sin_t, cos_t = sin_poly(theta, t2), cos_poly(t2)
    b1, b2, b3, b4 = (azimuth >= edge for edge in (45, 135, 225, 315))
    zero, step = jnp.zeros_like(azimuth), jnp.full_like(azimuth, 90)
    base = jnp.where(b1, step, zero) + jnp.where(b2, step, zero) + jnp.where(b3, step, zero) + jnp.where(b4, step, zero)
    rest = (azimuth - base).astype(jnp.float32) * (math.pi / 180.0)
    r2 = rest * rest
    s, c = sin_poly(rest, r2), cos_poly(r2)
    odd = (base == 90) | (base == 270)
    sin_m = jnp.where(odd, c, s)
    cos_m = jnp.where(odd, s, c)
    sin_neg = (base == 180) | (base == 270)
    cos_neg = (base == 90) | (base == 180)
    sin_p = jnp.where(sin_neg, -sin_m, sin_m)
    cos_p = jnp.where(cos_neg, -cos_m, cos_m)
    return sin_t * cos_p, sin_t * sin_p, cos_t


def kernel(sizes, now, prev, vel, eps, dlt, tilt, azim, aper, wave_out, img_out,
           U, M, A, K, corr, P_, Q, PC, QC, R1, R2, R3, local, ssem, rsem, isem):
    ngx, X, Y, Z = sizes
    T = Y // 8
    shot, gx, gy = lax.axis_index("shot"), lax.axis_index("gx"), lax.axis_index("gy")
    has_l, has_r = gx > 0, gx < ngx - 1
    core = lax.rem(shot, 2)
    core_pair = shot + 1 - 2 * core
    z_pair = lax.rem(shot + 2, 4)
    left, right, other = gx - 1, gx + 1, 1 - gy
    dev_l, dev_r, dev_y = (shot, left, gy), (shot, right, gy), (shot, gx, other)
    dev_dl, dev_dr = (shot, left, other), (shot, right, other)
    dev_c, dev_z = (core_pair, gx, gy), (z_pair, gx, gy)
    y_send = PAD + (Y - 1) * (1 - gy)
    y_recv = PAD - 1 + (Y + 1) * (1 - gy)

    loads = [pltpu.make_async_copy(now.at[0], U.at[0, :, pl.ds(1, X), pl.ds(PAD, Y), :], local.at[0])]
    for i, ref in enumerate((tilt, azim)):
        loads.append(pltpu.make_async_copy(ref, A.at[i], local.at[1 + i]))
    for i, ref in enumerate((vel, eps, dlt)):
        loads.append(pltpu.make_async_copy(ref, M.at[i], local.at[3 + i]))
    loads.append(pltpu.make_async_copy(prev.at[0], U.at[1, :, pl.ds(1, X), pl.ds(PAD, Y), :], local.at[6]))
    for copy in loads:
        copy.start()

    barrier = pltpu.get_barrier_semaphore()

    def hello(dev):
        pl.semaphore_signal(barrier, inc=1, device_id=dev, device_id_type=MESH)

    for dev in (dev_y, dev_c, dev_z):
        hello(dev)

    @pl.when(has_l)
    def _():
        hello(dev_l)
        hello(dev_dl)

    @pl.when(has_r)
    def _():
        hello(dev_r)
        hello(dev_dr)

    zero_tile = jnp.zeros((8, Z), jnp.float32)

    def zero_rows(x, c):
        for par in range(2):
            for f in range(F):
                U[par, f, x, pl.ds(0, 8), :] = zero_tile
                U[par, f, x, pl.ds(PAD + Y, 8), :] = zero_tile
        return c

    lax.fori_loop(0, X + 2, zero_rows, 0)

    def zero_plane(x):
        for par in range(2):
            for f in range(F):
                for j in range(T):
                    U[par, f, x, pl.ds(PAD + 8 * j, 8), :] = zero_tile

    @pl.when(jnp.logical_not(has_l))
    def _():
        zero_plane(0)

    @pl.when(jnp.logical_not(has_r))
    def _():
        zero_plane(X + 1)

    pl.semaphore_wait(barrier, 3 + 2 * has_l.astype(jnp.int32) + 2 * has_r.astype(jnp.int32))

    def halo(t, d):
        par = t % 2

        def plane(x):
            if t == 0:
                return now.at[0, :, x - 1]
            return U.at[par, :, x, pl.ds(PAD, Y), :]

        def make(d, src, dst, dev):
            return pltpu.make_async_remote_copy(
                src_ref=src, dst_ref=dst, send_sem=ssem.at[t, d], recv_sem=rsem.at[t, d],
                device_id=dev, device_id_type=MESH)

        if d == 0:
            return make(0, plane(1), U.at[par, :, X + 1, pl.ds(PAD, Y), :], dev_l)
        if d == 1:
            return make(1, plane(X), U.at[par, :, 0, pl.ds(PAD, Y), :], dev_r)
        if d == 2:
            return make(2, P_.at[t], Q.at[t], dev_y)
        if d == 3:
            return make(3, PC.at[t, 0], QC.at[t, 1], dev_dl)
        return make(4, PC.at[t, 1], QC.at[t, 0], dev_dr)

    def send_x(t):
        @pl.when(has_l)
        def _():
            halo(t, 0).start()

        @pl.when(has_r)
        def _():
            halo(t, 1).start()

    def send_y(t):
        par = t % 2
        for f in range(F):
            PC[t, 0, pl.ds(f, 1), :] = U[par, f, 1, pl.ds(y_send, 1), :]
            PC[t, 1, pl.ds(f, 1), :] = U[par, f, X, pl.ds(y_send, 1), :]

        @pl.when(has_l)
        def _():
            halo(t, 3).start()

        @pl.when(has_r)
        def _():
            halo(t, 4).start()

        for f in range(F):
            P_[t, f] = U[par, f, pl.ds(1, X), y_send, :]
        halo(t, 2).start()

    def receive_y(t):
        par = t % 2
        halo(t, 2).wait_recv()
        for f in range(F):
            U[par, f, pl.ds(1, X), y_recv, :] = Q[t, f]

    def receive_x(t):
        par = t % 2

        @pl.when(has_r)
        def _():
            halo(t, 0).wait_recv()
            halo(t, 3).wait_recv()
            for f in range(F):
                U[par, f, X + 1, pl.ds(y_recv, 1), :] = QC[t, 1, pl.ds(f, 1), :]

        @pl.when(has_l)
        def _():
            halo(t, 1).wait_recv()
            halo(t, 4).wait_recv()
            for f in range(F):
                U[par, f, 0, pl.ds(y_recv, 1), :] = QC[t, 0, pl.ds(f, 1), :]

    def sent(t):
        halo(t, 2).wait_send()

        @pl.when(has_l)
        def _():
            halo(t, 0).wait_send()
            halo(t, 3).wait_send()

        @pl.when(has_r)
        def _():
            halo(t, 1).wait_send()
            halo(t, 4).wait_send()

    send_x(0)
    loads[0].wait()
    send_y(0)

    lane = lax.broadcasted_iota(jnp.int32, (8, Z), 1)
    mask_p = jnp.where(lane == 0, 0.0, 1.0)
    mask_m = jnp.where(lane == Z - 1, 0.0, 1.0)
    for i in range(1, 6):
        loads[i].wait()

    def model(i, c):
        for n in range(2 * T):
            x, rows = 2 * i + n // T, pl.ds(8 * (n % T), 8)
            n_x, n_y, n_z = normals(A[0, x, rows, :], A[1, x, rows, :])
            v = M[0, x, rows, :]
            gain = 1.0 + 2.0 * M[1, x, rows, :]
            root = jnp.sqrt(1.0 + 2.0 * M[2, x, rows, :])
            half = 0.5 * n_z
            zz, xz, yz = n_z * n_z, half * n_x, half * n_y
            K[AXX, x, rows, :] = n_x * n_x
            K[AYY, x, rows, :] = n_y * n_y
            K[BXY, x, rows, :] = 0.5 * n_x * n_y
            for value, plus, minus in ((zz, AP, AM), (xz, BP, BM), (yz, CP, CM)):
                K[plus, x, rows, :] = pltpu.roll(value, 1, 1) * mask_p
                K[minus, x, rows, :] = pltpu.roll(value, Z - 1, 1) * mask_m
            K[CG, x, rows, :] = v * gain
            K[CR, x, rows, :] = v * root
            K[CV, x, rows, :] = v
        return c

    lax.fori_loop(0, X // 2, model, 0)
    loads[6].wait()
    covered = aper[0, 0, 0].astype(jnp.float32) * (1.0 / ITERS)

    edge_row = PAD + (Y - 8) * (1 - gy)
    inner_row = PAD + 8 * gy

    def group(t, x, row):
        a, b = t % 2, 1 - t % 2
        row = pl.multiple_of(row, 8)
        here, rows = pl.ds(row, 8), pl.ds(pl.multiple_of(row - PAD, 8), 8)
        k = [K[i, x - 1, rows, :] for i in range(NK)]
        cxx, cyy = 1.0 - k[AXX], 1.0 - k[AYY]
        cap, cam = mask_p - k[AP], mask_m - k[AM]
        centre, op, fresh = [], [], []
        for f in range(F):
            def at(off_x, off_y):
                return U[a, f, x + off_x, pl.ds(row + off_y, 8), :]

            m0, m1, m2 = at(-1, 0), at(0, 0), at(1, 0)
            up, down = at(0, 1), at(0, -1)
            dy, ys = up - down, up + down
            dx, xs = m2 - m0, m2 + m0
            dxy = (at(1, 1) - at(1, -1)) - (at(-1, 1) - at(-1, -1))
            tp = k[BP] * dx + k[CP] * dy
            tm = k[BM] * dx + k[CM] * dy
            mix = k[BXY] * dxy
            if f % 2 == 0:
                sp, sm = cap * m1 - tp, cam * m1 + tm
                side = cxx * xs + cyy * ys - mix
            else:
                sp, sm = k[AP] * m1 + tp, k[AM] * m1 - tm
                side = k[AXX] * xs + k[AYY] * ys + mix
            op.append(side + (pltpu.roll(sp, Z - 1, 1) + pltpu.roll(sm, 1, 1)))
            centre.append(m1)
        for pair in range(F // 2):
            fp, fq = 2 * pair, 2 * pair + 1
            p, q = centre[fp], centre[fq]
            p2, q2 = p + p, q + q
            across, along = op[fp] - (p2 + p2), op[fq] - q2
            p_new = (p2 - U[b, fp, x, here, :]) + (k[CG] * across + k[CR] * along)
            q_new = (q2 - U[b, fq, x, here, :]) + (k[CR] * across + k[CV] * along)
            if t == ITERS - 1:
                wave_out[0, fp, x - 1, rows, :] = p_new
                wave_out[0, fq, x - 1, rows, :] = q_new
            else:
                U[b, fp, x, here, :] = p_new
                U[b, fq, x, here, :] = q_new
            fresh.append(p_new)
        prod = fresh[0] * fresh[1]
        if t > 0:
            prod = prod + corr[x - 1, rows, :]
        if t == ITERS - 1:
            prod = prod * covered
        corr[x - 1, rows, :] = prod

    def interior(t):
        def body(i, c):
            for u in range(3):
                for k in range(T - 1):
                    group(t, 2 + 3 * i + u, inner_row + 8 * k)
            return c

        lax.fori_loop(0, (X - 2) // 3, body, 0)

    def y_edge(t):
        def body(i, c):
            for u in range(10):
                group(t, 2 + 10 * i + u, edge_row)
            return c

        lax.fori_loop(0, (X - 2) // 10, body, 0)

    def x_edges(t):
        for j in range(T):
            group(t, 1, PAD + 8 * j)
            group(t, X, PAD + 8 * j)

    H = X // 2
    in_rows = pl.ds(pl.multiple_of(8 * gy, 8), Y - 8)
    ed_rows = pl.ds(pl.multiple_of((Y - 8) * (1 - gy), 8), 8)

    def chunk(n, h):
        if n == 0:
            return pl.ds(1 + h * (H - 1), H - 1), in_rows
        if n == 1:
            return pl.ds(1 + h * (H - 1), H - 1), ed_rows
        return pl.ds(h * (X - 1), 1), pl.ds(0, Y)

    def image_copy(n, phase):
        mine, theirs = chunk(n, core), chunk(n, 1 - core)

        def make(src, dst, dev):
            return pltpu.make_async_remote_copy(
                src_ref=src, dst_ref=dst, send_sem=isem.at[0, phase, n], recv_sem=isem.at[1, phase, n],
                device_id=dev, device_id_type=MESH)

        if phase == 0:
            return make(corr.at[theirs], R1.at[theirs], dev_c)
        if phase == 1:
            return make(R1.at[mine], R2.at[mine], dev_z)
        return make(R3.at[mine], R3.at[mine], dev_c)

    def over(n, h, fn):
        xs, rows = chunk(n, h)

        def body(i, c):
            for j in range(rows.size // 8):
                fn(xs.start + i, pl.ds(pl.multiple_of(rows.start + 8 * j, 8), 8))
            return c

        if xs.size == 1:
            body(0, 0)
        else:
            lax.fori_loop(0, xs.size, body, 0)

    def image_chips(n):
        image_copy(n, 0).wait_recv()

        def add(x, rows):
            R1[x, rows, :] = R1[x, rows, :] + corr[x, rows, :]

        over(n, core, add)
        image_copy(n, 1).start()

    def image_gather(n):
        image_copy(n, 1).wait_recv()

        def add(x, rows):
            total = R1[x, rows, :] + R2[x, rows, :]
            R3[x, rows, :] = total
            img_out[x, rows, :] = total

        over(n, core, add)
        image_copy(n, 2).start()

    def image_finish(n):
        image_copy(n, 2).wait_recv()

        def put(x, rows):
            img_out[x, rows, :] = R3[x, rows, :]

        over(n, 1 - core, put)
        for phase in range(3):
            image_copy(n, phase).wait_send()

    last = ITERS - 1
    for t in range(ITERS):
        interior(t)
        if t == last:
            image_copy(0, 0).start()
        receive_y(t)
        if t > 0:
            sent(t - 1)
        y_edge(t)
        if t == last:
            image_copy(1, 0).start()
            image_chips(0)
        receive_x(t)
        x_edges(t)
        if t < last:
            send_x(t + 1)
            send_y(t + 1)
    image_copy(2, 0).start()
    image_chips(1)
    image_chips(2)
    for n in range(3):
        image_gather(n)
    for n in range(3):
        image_finish(n)
    sent(last)


def solution(mesh):
    ngx = mesh.shape["gx"]

    def local(now, prev, vel, eps, dlt, tilt, azim, aper):
        X, Y, Z = vel.shape
        hbm, vm = pl.BlockSpec(memory_space=pltpu.HBM), pltpu.VMEM
        f32 = jnp.float32
        return pl.pallas_call(
            functools.partial(kernel, (ngx, X, Y, Z)),
            out_shape=(jax.ShapeDtypeStruct(now.shape, f32), jax.ShapeDtypeStruct(vel.shape, f32)),
            in_specs=[hbm] * 7 + [pl.BlockSpec(memory_space=pltpu.SMEM)],
            out_specs=(pl.BlockSpec(memory_space=vm), pl.BlockSpec(memory_space=vm)),
            scratch_shapes=[
                vm((2, F, X + 2, Y + 2 * PAD, Z), f32),
                vm((3, X, Y, Z), f32),
                vm((2, X, Y, Z), jnp.int32),
                vm((NK, X, Y, Z), f32),
                vm((X, Y, Z), f32),
                vm((ITERS, F, X, Z), f32),
                vm((ITERS, F, X, Z), f32),
                vm((ITERS, 2, F, Z), f32),
                vm((ITERS, 2, F, Z), f32),
                vm((X, Y, Z), f32),
                vm((X, Y, Z), f32),
                vm((X, Y, Z), f32),
                pltpu.SemaphoreType.DMA((7,)),
                pltpu.SemaphoreType.DMA((ITERS, 5)),
                pltpu.SemaphoreType.DMA((ITERS, 5)),
                pltpu.SemaphoreType.DMA((2, 3, 3)),
            ],
            compiler_params=pltpu.CompilerParams(
                collective_id=0, has_side_effects=True, vmem_limit_bytes=58 * 1024 * 1024),
        )(now, prev, vel, eps, dlt, tilt, azim, aper)

    return jax.shard_map(
        local,
        mesh=mesh,
        in_specs=(
            P("shot", None, "gx", "gy", None),
            P("shot", None, "gx", "gy", None),
            P("gx", "gy", None),
            P("gx", "gy", None),
            P("gx", "gy", None),
            P("gx", "gy", None),
            P("gx", "gy", None),
            P("shot", "gx", "gy"),
        ),
        out_specs=(P("shot", None, "gx", "gy", None), P("gx", "gy", None)),
        check_vma=False,
    )
```

```python
import functools
import math

import jax
import jax.numpy as jnp
from jax import lax
from jax.experimental import pallas as pl
from jax.experimental.pallas import tpu as pltpu
from jax.sharding import PartitionSpec as P

ITERS = 4
F = 4
PAD = 8
MESH = pl.DeviceIdType.MESH
NK = 12
AXX, AYY, BXY, AP, AM, BP, BM, CP, CM, CG, CR, CV = range(NK)


def sin_poly(x, x2):
    return x * (1.0 + x2 * (-1.0 / 6 + x2 * (1.0 / 120 + x2 * (-1.0 / 5040 + x2 * (1.0 / 362880 + x2 * (-1.0 / 39916800 + x2 * (1.0 / 6227020800)))))))


def cos_poly(x2):
    return 1.0 + x2 * (-0.5 + x2 * (1.0 / 24 + x2 * (-1.0 / 720 + x2 * (1.0 / 40320 + x2 * (-1.0 / 3628800 + x2 * (1.0 / 479001600 - x2 * (1.0 / 87178291200)))))))


def normals(tilt, azimuth):
    theta = tilt.astype(jnp.float32) * (math.pi / 180.0)
    t2 = theta * theta
    sin_t, cos_t = sin_poly(theta, t2), cos_poly(t2)
    h = (azimuth - 180).astype(jnp.float32) * (math.pi / 360.0)
    h2 = h * h
    s, c = sin_poly(h, h2), cos_poly(h2)
    s2 = s + s
    return sin_t * (s2 * s - 1.0), -(sin_t * (s2 * c)), cos_t


def kernel(sizes, now, prev, vel, eps, dlt, tilt, azim, aper, wave_out, img_out,
           U, M, A, K, corr, P_, Q, PC, QC, QY, R1, R2, R3, D, local, ssem, rsem, isem, dsem, osem):
    ngx, X, Y, Z = sizes
    T = Y // 8
    shot, gx, gy = lax.axis_index("shot"), lax.axis_index("gx"), lax.axis_index("gy")
    has_l, has_r = gx > 0, gx < ngx - 1
    core = lax.rem(shot, 2)
    core_pair = shot + 1 - 2 * core
    z_pair = lax.rem(shot + 2, 4)
    other = 1 - gy
    dev_y = (shot, gx, other)
    dev_c, dev_z = (core_pair, gx, gy), (z_pair, gx, gy)
    dev_zc = (lax.rem(core_pair + 2, 4), gx, gy)
    first_side = (lax.rem(gx, 4) == 0).astype(jnp.int32)
    sides = (first_side, 1 - first_side)

    def has(side):
        return jnp.logical_or(jnp.logical_and(side == 0, has_l), jnp.logical_and(side == 1, has_r))
    y_send = PAD + (Y - 1) * (1 - gy)
    y_recv = PAD - 1 + (Y + 1) * (1 - gy)

    loads = []
    for i, ref in enumerate((tilt, azim)):
        loads.append(pltpu.make_async_copy(ref, A.at[i], local.at[i]))
    for i, ref in enumerate((vel, eps, dlt)):
        loads.append(pltpu.make_async_copy(ref, M.at[i], local.at[2 + i]))
    for i, ref in enumerate((now, prev)):
        loads.append(pltpu.make_async_copy(ref.at[0], U.at[i, :, pl.ds(1, X), pl.ds(PAD, Y), :], local.at[5 + i]))
    for copy in loads:
        copy.start()

    barrier = pltpu.get_barrier_semaphore()

    def hello(dev):
        pl.semaphore_signal(barrier, inc=1, device_id=dev, device_id_type=MESH)

    for dev in (dev_y, dev_c, dev_z, dev_zc):
        hello(dev)

    @pl.when(has_l)
    def _():
        hello((shot, gx - 1, gy))
        hello((shot, gx - 1, other))

    @pl.when(has_r)
    def _():
        hello((shot, gx + 1, gy))
        hello((shot, gx + 1, other))

    zero_tile = jnp.zeros((8, Z), jnp.float32)

    def zero_rows(x, c):
        for par in range(2):
            for f in range(F):
                U[par, f, x, pl.ds(0, 8), :] = zero_tile
                U[par, f, x, pl.ds(PAD + Y, 8), :] = zero_tile
        return c

    lax.fori_loop(0, X + 2, zero_rows, 0)

    def zero_plane(x):
        for par in range(2):
            for f in range(F):
                for j in range(T):
                    U[par, f, x, pl.ds(PAD + 8 * j, 8), :] = zero_tile

    @pl.when(jnp.logical_not(has_l))
    def _():
        zero_plane(0)

    @pl.when(jnp.logical_not(has_r))
    def _():
        zero_plane(X + 1)

    pl.semaphore_wait(barrier, 4 + 2 * has_l.astype(jnp.int32) + 2 * has_r.astype(jnp.int32))

    def x_copy(t, side):
        plane = 1 + side * (X - 1)
        return pltpu.make_async_remote_copy(
            src_ref=now.at[0, :, plane - 1] if t == 0 else U.at[t % 2, :, plane, pl.ds(PAD, Y), :],
            dst_ref=U.at[t % 2, :, (1 - side) * (X + 1), pl.ds(PAD, Y), :],
            send_sem=ssem.at[t, side], recv_sem=rsem.at[t, 1 - side],
            device_id=(shot, gx + 2 * side - 1, gy), device_id_type=MESH)

    y_line = (Y - 1) * (1 - gy)

    def corner_copy(t, side):
        return pltpu.make_async_remote_copy(
            src_ref=now.at[0, :, side * (X - 1), y_line, :] if t == 0 else PC.at[t, side], dst_ref=QC.at[t, 1 - side],
            send_sem=ssem.at[t, 3 + side], recv_sem=rsem.at[t, 4 - side],
            device_id=(shot, gx + 2 * side - 1, other), device_id_type=MESH)

    def y_copy(t):
        return pltpu.make_async_remote_copy(
            src_ref=now.at[0, :, :, y_line, :] if t == 0 else P_.at[t], dst_ref=Q.at[t],
            send_sem=ssem.at[t, 2], recv_sem=rsem.at[t, 2], device_id=dev_y, device_id_type=MESH)

    def y_end_copy(t, side):
        return pltpu.make_async_remote_copy(
            src_ref=PC.at[t, side], dst_ref=QY.at[t, side], send_sem=ssem.at[t, 5 + side], recv_sem=rsem.at[t, 5 + side],
            device_id=dev_y, device_id_type=MESH)

    def send_x(t, side):
        @pl.when(has(side))
        def _():
            x_copy(t, side).start()

    def send_corner(t, side):
        if t > 0:
            for f in range(F):
                PC[t, side, pl.ds(f, 1), :] = U[t % 2, f, 1 + side * (X - 1), pl.ds(y_send, 1), :]
            y_end_copy(t, side).start()

        @pl.when(has(side))
        def _():
            corner_copy(t, side).start()

    def send_y(t):
        if t > 0:
            for f in range(F):
                P_[t, f] = U[t % 2, f, pl.ds(1, X), y_send, :]
        y_copy(t).start()

    def receive_y(t):
        y_copy(t).wait_recv()
        for f in range(F):
            U[t % 2, f, pl.ds(1, X), y_recv, :] = Q[t, f]
        if t > 0:
            for side in range(2):
                y_end_copy(t, side).wait_recv()
                for f in range(F):
                    U[t % 2, f, 1 + side * (X - 1), pl.ds(y_recv, 1), :] = QY[t, side, pl.ds(f, 1), :]

    def receive_x(t, side):
        @pl.when(has(side))
        def _():
            x_copy(t, 1 - side).wait_recv()
            corner_copy(t, 1 - side).wait_recv()
            for f in range(F):
                U[t % 2, f, side * (X + 1), pl.ds(y_recv, 1), :] = QC[t, side, pl.ds(f, 1), :]

    def sent(t, side):
        @pl.when(has(side))
        def _():
            x_copy(t, side).wait_send()
            corner_copy(t, side).wait_send()

    send_y(0)
    for side in sides:
        send_x(0, side)
        send_corner(0, side)

    lane = lax.broadcasted_iota(jnp.int32, (8, Z), 1)
    mask_p = jnp.where(lane == 0, 0.0, 1.0)
    mask_m = jnp.where(lane == Z - 1, 0.0, 1.0)
    for i in range(5):
        loads[i].wait()

    def model(i, c):
        for n in range(4 * T):
            x, rows = 4 * i + n // T, pl.ds(8 * (n % T), 8)
            n_x, n_y, n_z = normals(A[0, x, rows, :], A[1, x, rows, :])
            v = M[0, x, rows, :]
            gain = 1.0 + 2.0 * M[1, x, rows, :]
            root = jnp.sqrt(1.0 + 2.0 * M[2, x, rows, :])
            half = 0.5 * n_z
            zz, xz, yz = n_z * n_z, half * n_x, half * n_y
            K[AXX, x, rows, :] = n_x * n_x
            K[AYY, x, rows, :] = n_y * n_y
            K[BXY, x, rows, :] = 0.5 * n_x * n_y
            for value, plus, minus in ((zz, AP, AM), (xz, BP, BM), (yz, CP, CM)):
                K[plus, x, rows, :] = pltpu.roll(value, 1, 1) * mask_p
                K[minus, x, rows, :] = pltpu.roll(value, Z - 1, 1) * mask_m
            K[CG, x, rows, :] = v * gain
            K[CR, x, rows, :] = v * root
            K[CV, x, rows, :] = v
        return c

    lax.fori_loop(0, X // 4, model, 0)
    loads[5].wait()
    loads[6].wait()
    covered = aper[0, 0, 0].astype(jnp.float32) * (1.0 / ITERS)

    edge_row = PAD + (Y - 8) * (1 - gy)
    inner_row = PAD + 8 * gy

    def group(t, x, row, edge=None):
        a, b = t % 2, 1 - t % 2
        row = pl.multiple_of(row, 8)
        here, rows = pl.ds(row, 8), pl.ds(pl.multiple_of(row - PAD, 8), 8)
        k = [K[i, x - 1, rows, :] for i in range(NK)]
        cxx, cyy = 1.0 - k[AXX], 1.0 - k[AYY]
        cap, cam = mask_p - k[AP], mask_m - k[AM]
        centre, op, fresh = [], [], []
        for f in range(F):
            def at(off_x, off_y):
                return U[a, f, x + off_x, pl.ds(row + off_y, 8), :]

            m0, m1, m2 = at(-1, 0), at(0, 0), at(1, 0)
            up, down = at(0, 1), at(0, -1)
            dy, ys = up - down, up + down
            dx, xs = m2 - m0, m2 + m0
            dxy = (at(1, 1) - at(1, -1)) - (at(-1, 1) - at(-1, -1))
            tp = k[BP] * dx + k[CP] * dy
            tm = k[BM] * dx + k[CM] * dy
            mix = k[BXY] * dxy
            if f % 2 == 0:
                sp, sm = cap * m1 - tp, cam * m1 + tm
                side = cxx * xs + cyy * ys - mix
            else:
                sp, sm = k[AP] * m1 + tp, k[AM] * m1 - tm
                side = k[AXX] * xs + k[AYY] * ys + mix
            op.append(side + (pltpu.roll(sp, Z - 1, 1) + pltpu.roll(sm, 1, 1)))
            centre.append(m1)
        for pair in range(F // 2):
            fp, fq = 2 * pair, 2 * pair + 1
            p, q = centre[fp], centre[fq]
            p2, q2 = p + p, q + q
            across, along = op[fp] - (p2 + p2), op[fq] - q2
            p_new = (p2 - U[b, fp, x, here, :]) + (k[CG] * across + k[CR] * along)
            q_new = (q2 - U[b, fq, x, here, :]) + (k[CR] * across + k[CV] * along)
            U[b, fp, x, here, :] = p_new
            U[b, fq, x, here, :] = q_new
            fresh.append(p_new)
        prod = fresh[0] * fresh[1]
        if t > 0:
            prod = prod + corr[x - 1, rows, :]
        if t == ITERS - 1:
            prod = prod * covered
        if t == ITERS - 1 and edge is not None:
            D[shot, edge, rows, :] = prod
        else:
            corr[x - 1, rows, :] = prod

    far_row = PAD + 16 * gy
    near_row = PAD + Y - 16 - (Y - 24) * gy

    def interior(t):
        def body(i, c):
            for u in range(3):
                for k in range(T - 1):
                    group(t, 2 + 3 * i + u, inner_row + 8 * k)
            return c

        lax.fori_loop(0, (X - 2) // 3, body, 0)

    def core_part(t):
        def body(i, c):
            for u in range(4):
                for k in range(T - 2):
                    group(t, 3 + 4 * i + u, far_row + 8 * k)
            return c

        lax.fori_loop(0, (X - 4) // 4, body, 0)

    def rest_part(t):
        for x in (2, X - 1):
            for k in range(T - 2):
                group(t, x, far_row + 8 * k)

        def body(i, c):
            for u in range(10):
                group(t, 2 + 10 * i + u, near_row)
            return c

        lax.fori_loop(0, (X - 2) // 10, body, 0)

    def y_edge(t):
        def body(i, c):
            for u in range(10):
                group(t, 2 + 10 * i + u, edge_row)
            return c

        lax.fori_loop(0, (X - 2) // 10, body, 0)

    def x_edge(t, side):
        for j in range(T):
            group(t, 1 + side * (X - 1), PAD + 8 * j, side)

    far = pl.ds(pl.multiple_of(16 * gy, 8), 8 * (T - 2))
    near = pl.ds(pl.multiple_of(Y - 16 - (Y - 24) * gy, 8), 8)
    edge_rows = pl.ds(pl.multiple_of((Y - 8) * (1 - gy), 8), 8)
    CHUNKS = ((2, (X - 4) // 2, (X - 4) // 2, far), (1, X // 2 - 1, X // 2 - 1, near), (1, X // 2 - 1, X // 2 - 1, edge_rows), (1, X - 3, 1, far))
    NC = len(CHUNKS)

    def chunk(n, h):
        low, hop, count, rows = CHUNKS[n]
        return pl.ds(low + h * hop, count), rows

    def image_copy(n, phase):
        mine, theirs = chunk(n, core), chunk(n, 1 - core)

        def make(src, dst, dev):
            return pltpu.make_async_remote_copy(
                src_ref=src, dst_ref=dst, send_sem=isem.at[0, phase, n], recv_sem=isem.at[1, phase, n],
                device_id=dev, device_id_type=MESH)

        if phase == 0:
            return make(corr.at[theirs], R1.at[theirs], dev_c)
        if phase == 1:
            return make(R1.at[mine], R2.at[mine], dev_z)
        return make(R3.at[mine], R3.at[mine], dev_c)

    def over(n, h, fn):
        xs, rows = chunk(n, h)

        def body(i, c):
            for j in range(rows.size // 8):
                fn(xs.start + i, pl.ds(pl.multiple_of(rows.start + 8 * j, 8), 8))
            return c

        if xs.size == 1:
            body(0, 0)
        else:
            lax.fori_loop(0, xs.size, body, 0)

    def image_chips(n):
        image_copy(n, 0).wait_recv()

        def add(x, rows):
            R1[x, rows, :] = R1[x, rows, :] + corr[x, rows, :]

        over(n, core, add)
        image_copy(n, 1).start()

    def image_gather(n):
        image_copy(n, 1).wait_recv()

        def add(x, rows):
            R3[x, rows, :] = R1[x, rows, :] + R2[x, rows, :]

        over(n, core, add)
        image_copy(n, 2).start()

    def out_copy(n, h):
        xs, rows = chunk(n, h)
        return pltpu.make_async_copy(R3.at[xs, rows, :], img_out.at[xs, rows, :], osem.at[n, h])

    def image_finish(n):
        out_copy(n, core).start()
        image_copy(n, 2).wait_recv()
        out_copy(n, 1 - core).start()

    def edge_out(side):
        plane = side * (X - 1)
        return pltpu.make_async_copy(R3.at[plane], img_out.at[plane], osem.at[4, side])

    peers = (dev_c, dev_z, dev_zc)

    def direct(i, side, slot):
        return pltpu.make_async_remote_copy(
            src_ref=D.at[slot, side], dst_ref=D.at[slot, side], send_sem=dsem.at[0, i, side], recv_sem=dsem.at[1, slot, side],
            device_id=peers[i], device_id_type=MESH)

    last = ITERS - 1
    for t in range(ITERS):
        if t == 1:
            interior(0)
        if t == last:
            image_chips(0)
            rest_part(t)
            image_copy(1, 0).start()
            image_copy(3, 0).start()
            image_chips(1)
            image_chips(3)
        elif t > 0:
            interior(t)
        if t == last - 1:
            core_part(last)
            image_copy(0, 0).start()
        receive_y(t)
        y_edge(t)
        if t < last:
            send_y(t + 1)
        else:
            image_copy(2, 0).start()
        for side in sides:
            receive_x(t, side)
            if t > 0:
                sent(t - 1, side)
            x_edge(t, side)
            if t < last:
                send_x(t + 1, side)
                send_corner(t + 1, side)
            else:
                for i in (1, 2, 0):
                    direct(i, side, shot).start()
    image_chips(2)
    wave_copy = pltpu.make_async_copy(U.at[ITERS % 2, :, pl.ds(1, X), pl.ds(PAD, Y), :], wave_out.at[0], osem.at[5, 0])
    wave_copy.start()
    for n in (0, 1, 3):
        image_gather(n)
    for n in (0, 1, 3):
        image_finish(n)
    image_gather(2)
    for side in sides:
        for i, slot in enumerate((core_pair, z_pair, lax.rem(core_pair + 2, 4))):
            direct(i, side, slot).wait_recv()
        for j in range(T):
            rows = pl.ds(8 * j, 8)
            total = (D[0, side, rows, :] + D[1, side, rows, :]) + (D[2, side, rows, :] + D[3, side, rows, :])
            R3[side * (X - 1), rows, :] = total
        edge_out(side).start()
    image_finish(2)
    for n in range(NC):
        for phase in range(3):
            image_copy(n, phase).wait_send()
    for side in sides:
        sent(last, side)
        for i in range(3):
            direct(i, side, shot).wait_send()
        for t in range(1, ITERS):
            y_end_copy(t, side).wait_send()
    for t in range(ITERS):
        y_copy(t).wait_send()
    for n in range(NC):
        for h in range(2):
            out_copy(n, h).wait()
    for side in sides:
        edge_out(side).wait()
    wave_copy.wait()


def hand_over(wave, image, wave_out, image_out, wave_buf, image_buf, sem):
    parts = [(wave.at[0, f, pl.ds(h * 16, 16)], wave_buf.at[f, pl.ds(h * 16, 16)], wave_out.at[0, f, pl.ds(h * 16, 16)]) for f in range(F) for h in range(2)]
    parts.append((image, image_buf, image_out))
    reads = [pltpu.make_async_copy(src, buf, sem.at[0, n]) for n, (src, buf, _) in enumerate(parts)]
    writes = [pltpu.make_async_copy(buf, dst, sem.at[1, n]) for n, (_, buf, dst) in enumerate(parts)]
    for copy in reads:
        copy.start()
    for read, write in zip(reads, writes):
        read.wait()
        write.start()
    for copy in writes:
        copy.wait()


def solution(mesh):
    ngx = mesh.shape["gx"]

    def local(now, prev, vel, eps, dlt, tilt, azim, aper):
        X, Y, Z = vel.shape
        hbm, vm = pl.BlockSpec(memory_space=pltpu.HBM), pltpu.VMEM
        f32 = jnp.float32
        wave, image = pl.pallas_call(
            functools.partial(kernel, (ngx, X, Y, Z)),
            out_shape=(jax.ShapeDtypeStruct(now.shape, f32), jax.ShapeDtypeStruct(vel.shape, f32)),
            in_specs=[hbm] * 7 + [pl.BlockSpec(memory_space=pltpu.SMEM)],
            out_specs=(hbm, hbm),
            scratch_shapes=[
                vm((2, F, X + 2, Y + 2 * PAD, Z), f32),
                vm((3, X, Y, Z), f32),
                vm((2, X, Y, Z), jnp.int32),
                vm((NK, X, Y, Z), f32),
                vm((X, Y, Z), f32),
                vm((ITERS, F, X, Z), f32),
                vm((ITERS, F, X, Z), f32),
                vm((ITERS, 2, F, Z), f32),
                vm((ITERS, 2, F, Z), f32),
                vm((ITERS, 2, F, Z), f32),
                vm((X, Y, Z), f32),
                vm((X, Y, Z), f32),
                vm((X, Y, Z), f32),
                vm((4, 2, Y, Z), f32),
                pltpu.SemaphoreType.DMA((7,)),
                pltpu.SemaphoreType.DMA((ITERS, 7)),
                pltpu.SemaphoreType.DMA((ITERS, 7)),
                pltpu.SemaphoreType.DMA((2, 3, 4)),
                pltpu.SemaphoreType.DMA((2, 4, 2)),
                pltpu.SemaphoreType.DMA((6, 2)),
            ],
            compiler_params=pltpu.CompilerParams(
                collective_id=0, has_side_effects=True, vmem_limit_bytes=58 * 1024 * 1024),
        )(now, prev, vel, eps, dlt, tilt, azim, aper)
        return pl.pallas_call(
            hand_over,
            out_shape=(jax.ShapeDtypeStruct(now.shape, f32), jax.ShapeDtypeStruct(vel.shape, f32)),
            in_specs=[hbm] * 2,
            out_specs=(hbm, hbm),
            scratch_shapes=[vm(now.shape[1:], f32), vm(vel.shape, f32), pltpu.SemaphoreType.DMA((2, 2 * F + 1))],
            compiler_params=pltpu.CompilerParams(vmem_limit_bytes=58 * 1024 * 1024),
        )(wave, image)

    return jax.shard_map(
        local,
        mesh=mesh,
        in_specs=(
            P("shot", None, "gx", "gy", None),
            P("shot", None, "gx", "gy", None),
            P("gx", "gy", None),
            P("gx", "gy", None),
            P("gx", "gy", None),
            P("gx", "gy", None),
            P("gx", "gy", None),
            P("shot", "gx", "gy"),
        ),
        out_specs=(P("shot", None, "gx", "gy", None), P("gx", "gy", None)),
        check_vma=False,
    )
```

```python
import functools
import math

import jax
import jax.numpy as jnp
from jax import lax
from jax.experimental import pallas as pl
from jax.experimental.pallas import tpu as pltpu
from jax.sharding import PartitionSpec as P

ITERS = 4
F = 4
PAD = 8
MESH = pl.DeviceIdType.MESH
NK = 12
AXX, AYY, BXY, AP, AM, BP, BM, CP, CM, CG, CR, CV = range(NK)


def sin_poly(x, x2):
    return x * (1.0 + x2 * (-1.0 / 6 + x2 * (1.0 / 120 + x2 * (-1.0 / 5040 + x2 * (1.0 / 362880 + x2 * (-1.0 / 39916800 + x2 * (1.0 / 6227020800)))))))


def cos_poly(x2):
    return 1.0 + x2 * (-0.5 + x2 * (1.0 / 24 + x2 * (-1.0 / 720 + x2 * (1.0 / 40320 + x2 * (-1.0 / 3628800 + x2 * (1.0 / 479001600 - x2 * (1.0 / 87178291200)))))))


def normals(tilt, azimuth):
    theta = tilt.astype(jnp.float32) * (math.pi / 180.0)
    t2 = theta * theta
    sin_t, cos_t = sin_poly(theta, t2), cos_poly(t2)
    h = (azimuth - 180).astype(jnp.float32) * (math.pi / 360.0)
    h2 = h * h
    s, c = sin_poly(h, h2), cos_poly(h2)
    s2 = s + s
    return sin_t * (s2 * s - 1.0), -(sin_t * (s2 * c)), cos_t


def kernel(sizes, now, prev, vel, eps, dlt, tilt, azim, aper, wave_out, img_out,
           U, M, A, K, corr, early, P_, Q, PC, QC, QY, R1, R2, R3, D, line, local, ssem, rsem, isem, dsem, osem):
    ngx, X, Y, Z = sizes
    T = Y // 8
    shot, gx, gy = lax.axis_index("shot"), lax.axis_index("gx"), lax.axis_index("gy")
    has_l, has_r = gx > 0, gx < ngx - 1
    core = lax.rem(shot, 2)
    core_pair = shot + 1 - 2 * core
    z_pair = lax.rem(shot + 2, 4)
    other = 1 - gy
    dev_y = (shot, gx, other)
    dev_c, dev_z = (core_pair, gx, gy), (z_pair, gx, gy)
    dev_zc = (lax.rem(core_pair + 2, 4), gx, gy)
    first_side = (lax.rem(gx, 4) == 0).astype(jnp.int32)
    sides = (first_side, 1 - first_side)

    def has(side):
        return jnp.logical_or(jnp.logical_and(side == 0, has_l), jnp.logical_and(side == 1, has_r))
    y_send = PAD + (Y - 1) * (1 - gy)
    y_recv = PAD - 1 + (Y + 1) * (1 - gy)

    loads = []
    for i, ref in enumerate((tilt, azim)):
        loads.append(pltpu.make_async_copy(ref, A.at[i], local.at[i]))
    for i, ref in enumerate((vel, eps, dlt)):
        loads.append(pltpu.make_async_copy(ref, M.at[i], local.at[2 + i]))
    for i, ref in enumerate((now, prev)):
        loads.append(pltpu.make_async_copy(ref.at[0], U.at[i, :, pl.ds(1, X), pl.ds(PAD, Y), :], local.at[5 + i]))
    for copy in loads:
        copy.start()

    barrier = pltpu.get_barrier_semaphore()

    def hello(dev):
        pl.semaphore_signal(barrier, inc=1, device_id=dev, device_id_type=MESH)

    for dev in (dev_y, dev_c, dev_z, dev_zc):
        hello(dev)

    @pl.when(has_l)
    def _():
        hello((shot, gx - 1, gy))
        hello((shot, gx - 1, other))

    @pl.when(has_r)
    def _():
        hello((shot, gx + 1, gy))
        hello((shot, gx + 1, other))

    zero_tile = jnp.zeros((8, Z), jnp.float32)

    def zero_rows(x, c):
        for par in range(2):
            for f in range(F):
                U[par, f, x, pl.ds(0, 8), :] = zero_tile
                U[par, f, x, pl.ds(PAD + Y, 8), :] = zero_tile
        return c

    lax.fori_loop(0, X + 2, zero_rows, 0)

    def zero_plane(x):
        for par in range(2):
            for f in range(F):
                for j in range(T):
                    U[par, f, x, pl.ds(PAD + 8 * j, 8), :] = zero_tile

    @pl.when(jnp.logical_not(has_l))
    def _():
        zero_plane(0)

    @pl.when(jnp.logical_not(has_r))
    def _():
        zero_plane(X + 1)

    pl.semaphore_wait(barrier, 4 + 2 * has_l.astype(jnp.int32) + 2 * has_r.astype(jnp.int32))

    def x_copy(t, side):
        plane = 1 + side * (X - 1)
        return pltpu.make_async_remote_copy(
            src_ref=now.at[0, :, plane - 1] if t == 0 else U.at[t % 2, :, plane, pl.ds(PAD, Y), :],
            dst_ref=U.at[t % 2, :, (1 - side) * (X + 1), pl.ds(PAD, Y), :],
            send_sem=ssem.at[t, side], recv_sem=rsem.at[t, 1 - side],
            device_id=(shot, gx + 2 * side - 1, gy), device_id_type=MESH)

    y_line = (Y - 1) * (1 - gy)

    def corner_copy(t, side):
        return pltpu.make_async_remote_copy(
            src_ref=now.at[0, :, side * (X - 1), y_line, :] if t == 0 else PC.at[t, side], dst_ref=QC.at[t, 1 - side],
            send_sem=ssem.at[t, 3 + side], recv_sem=rsem.at[t, 4 - side],
            device_id=(shot, gx + 2 * side - 1, other), device_id_type=MESH)

    def y_copy(t):
        return pltpu.make_async_remote_copy(
            src_ref=now.at[0, :, :, y_line, :] if t == 0 else P_.at[t], dst_ref=Q.at[t],
            send_sem=ssem.at[t, 2], recv_sem=rsem.at[t, 2], device_id=dev_y, device_id_type=MESH)

    def y_end_copy(t, side):
        return pltpu.make_async_remote_copy(
            src_ref=PC.at[t, side], dst_ref=QY.at[t, side], send_sem=ssem.at[t, 5 + side], recv_sem=rsem.at[t, 5 + side],
            device_id=dev_y, device_id_type=MESH)

    def send_x(t, side):
        @pl.when(has(side))
        def _():
            x_copy(t, side).start()

    def send_corner(t, side):
        if t > 0:
            for f in range(F):
                PC[t, side, pl.ds(f, 1), :] = U[t % 2, f, 1 + side * (X - 1), pl.ds(y_send, 1), :]
            y_end_copy(t, side).start()

        @pl.when(has(side))
        def _():
            corner_copy(t, side).start()

    def send_y(t):
        if t > 0:
            for f in range(F):
                P_[t, f] = U[t % 2, f, pl.ds(1, X), y_send, :]
        y_copy(t).start()

    def receive_y(t):
        y_copy(t).wait_recv()
        for f in range(F):
            U[t % 2, f, pl.ds(1, X), y_recv, :] = Q[t, f]
        if t > 0:
            for side in range(2):
                y_end_copy(t, side).wait_recv()
                for f in range(F):
                    U[t % 2, f, 1 + side * (X - 1), pl.ds(y_recv, 1), :] = QY[t, side, pl.ds(f, 1), :]

    def receive_x(t, side):
        @pl.when(has(side))
        def _():
            x_copy(t, 1 - side).wait_recv()

    def receive_corner(t, side):
        @pl.when(has(side))
        def _():
            corner_copy(t, 1 - side).wait_recv()
            for f in range(F):
                U[t % 2, f, side * (X + 1), pl.ds(y_recv, 1), :] = QC[t, side, pl.ds(f, 1), :]

    def sent(t, side):
        @pl.when(has(side))
        def _():
            x_copy(t, side).wait_send()
            corner_copy(t, side).wait_send()

    send_y(0)
    for side in sides:
        send_corner(0, side)
        send_x(0, side)

    lane = lax.broadcasted_iota(jnp.int32, (8, Z), 1)
    mask_p = jnp.where(lane == 0, 0.0, 1.0)
    mask_m = jnp.where(lane == Z - 1, 0.0, 1.0)
    for i in range(5):
        loads[i].wait()

    def model(i, c):
        for n in range(4 * T):
            x, rows = 4 * i + n // T, pl.ds(8 * (n % T), 8)
            n_x, n_y, n_z = normals(A[0, x, rows, :], A[1, x, rows, :])
            v = M[0, x, rows, :]
            gain = 1.0 + 2.0 * M[1, x, rows, :]
            root = jnp.sqrt(1.0 + 2.0 * M[2, x, rows, :])
            half = 0.5 * n_z
            zz, xz, yz = n_z * n_z, half * n_x, half * n_y
            K[AXX, x, rows, :] = n_x * n_x
            K[AYY, x, rows, :] = n_y * n_y
            K[BXY, x, rows, :] = 0.5 * n_x * n_y
            for value, plus, minus in ((zz, AP, AM), (xz, BP, BM), (yz, CP, CM)):
                K[plus, x, rows, :] = pltpu.roll(value, 1, 1) * mask_p
                K[minus, x, rows, :] = pltpu.roll(value, Z - 1, 1) * mask_m
            K[CG, x, rows, :] = v * gain
            K[CR, x, rows, :] = v * root
            K[CV, x, rows, :] = v
        return c

    lax.fori_loop(0, X // 4, model, 0)
    loads[5].wait()
    loads[6].wait()
    covered = aper[0, 0, 0].astype(jnp.float32) * (1.0 / ITERS)

    edge_row = PAD + (Y - 8) * (1 - gy)
    inner_row = PAD + 8 * gy

    def group(t, x, row, edge=None, ahead=False):
        a, b = t % 2, 1 - t % 2
        row = pl.multiple_of(row, 8)
        here, rows = pl.ds(row, 8), pl.ds(pl.multiple_of(row - PAD, 8), 8)
        k = [K[i, x - 1, rows, :] for i in range(NK)]
        cxx, cyy = 1.0 - k[AXX], 1.0 - k[AYY]
        cap, cam = mask_p - k[AP], mask_m - k[AM]
        centre, op, fresh = [], [], []
        for f in range(F):
            def at(off_x, off_y):
                return U[a, f, x + off_x, pl.ds(row + off_y, 8), :]

            m0, m1, m2 = at(-1, 0), at(0, 0), at(1, 0)
            up, down = at(0, 1), at(0, -1)
            dy, ys = up - down, up + down
            dx, xs = m2 - m0, m2 + m0
            dxy = (at(1, 1) - at(1, -1)) - (at(-1, 1) - at(-1, -1))
            tp = k[BP] * dx + k[CP] * dy
            tm = k[BM] * dx + k[CM] * dy
            mix = k[BXY] * dxy
            if f % 2 == 0:
                sp, sm = cap * m1 - tp, cam * m1 + tm
                side = cxx * xs + cyy * ys - mix
            else:
                sp, sm = k[AP] * m1 + tp, k[AM] * m1 - tm
                side = k[AXX] * xs + k[AYY] * ys + mix
            op.append(side + (pltpu.roll(sp, Z - 1, 1) + pltpu.roll(sm, 1, 1)))
            centre.append(m1)
        for pair in range(F // 2):
            fp, fq = 2 * pair, 2 * pair + 1
            p, q = centre[fp], centre[fq]
            p2, q2 = p + p, q + q
            across, along = op[fp] - (p2 + p2), op[fq] - q2
            p_new = (p2 - U[b, fp, x, here, :]) + (k[CG] * across + k[CR] * along)
            q_new = (q2 - U[b, fq, x, here, :]) + (k[CR] * across + k[CV] * along)
            if not ahead:
                U[b, fp, x, here, :] = p_new
                U[b, fq, x, here, :] = q_new
            fresh.append(p_new)
        prod = fresh[0] * fresh[1]
        if t > 0:
            prod = prod + corr[x - 1, rows, :]
        if t == ITERS - 1:
            prod = prod * covered
        if t == ITERS - 1 and edge is not None:
            D[shot, edge, rows, :] = prod
        elif ahead:
            early[x - 1] = prod
        else:
            corr[x - 1, rows, :] = prod

    far_row = PAD + 16 * gy
    near_row = PAD + Y - 16 - (Y - 24) * gy

    def interior(t):
        def body(i, c):
            for u in range(3):
                for k in range(T - 1):
                    group(t, 2 + 3 * i + u, inner_row + 8 * k)
            return c

        lax.fori_loop(0, (X - 2) // 3, body, 0)

    def core_part(t):
        def body(i, c):
            for u in range(4):
                for k in range(T - 2):
                    group(t, 3 + 4 * i + u, far_row + 8 * k)
            return c

        lax.fori_loop(0, (X - 4) // 4, body, 0)

    def rest_part(t):
        for x in (2, X - 1):
            for k in range(T - 2):
                group(t, x, far_row + 8 * k)

        def body(i, c):
            for u in range(10):
                group(t, 2 + 10 * i + u, near_row)
            return c

        lax.fori_loop(0, (X - 2) // 10, body, 0)

    def y_edge(t, ahead=False):
        def body(i, c):
            for u in range(10):
                group(t, 2 + 10 * i + u, edge_row, ahead=ahead)
            return c

        lax.fori_loop(0, (X - 2) // 10, body, 0)

    def x_edge(t, side):
        plane = 1 + side * (X - 1)
        for k in range(T - 1):
            group(t, plane, inner_row + 8 * k, side)
        receive_corner(t, side)
        group(t, plane, edge_row, side)

    far = pl.ds(pl.multiple_of(16 * gy, 8), 8 * (T - 2))
    near = pl.ds(pl.multiple_of(Y - 16 - (Y - 24) * gy, 8), 8)
    edge_rows = pl.ds(pl.multiple_of((Y - 8) * (1 - gy), 8), 8)
    CHUNKS = ((2, (X - 4) // 2, (X - 4) // 2, far), (1, X // 2 - 1, X // 2 - 1, near), (1, X // 2 - 1, X // 2 - 1, edge_rows), (1, X - 3, 1, far))
    NC = len(CHUNKS)

    def chunk(n, h):
        low, hop, count, rows = CHUNKS[n]
        return pl.ds(low + h * hop, count), rows

    def image_copy(n, phase):
        mine, theirs = chunk(n, core), chunk(n, 1 - core)

        def make(src, dst, dev):
            return pltpu.make_async_remote_copy(
                src_ref=src, dst_ref=dst, send_sem=isem.at[0, phase, n], recv_sem=isem.at[1, phase, n],
                device_id=dev, device_id_type=MESH)

        if phase == 0:
            return make(early.at[theirs[0]] if n == 2 else corr.at[theirs], R1.at[theirs], dev_c)
        if phase == 1:
            return make(R1.at[mine], R2.at[mine], dev_z)
        return make(R3.at[mine], R3.at[mine], dev_c)

    def over(n, h, fn):
        xs, rows = chunk(n, h)

        def body(i, c):
            for j in range(rows.size // 8):
                fn(xs.start + i, pl.ds(pl.multiple_of(rows.start + 8 * j, 8), 8))
            return c

        if xs.size == 1:
            body(0, 0)
        else:
            lax.fori_loop(0, xs.size, body, 0)

    def image_chips(n):
        image_copy(n, 0).wait_recv()

        def add(x, rows):
            R1[x, rows, :] = R1[x, rows, :] + (early[x] if n == 2 else corr[x, rows, :])

        over(n, core, add)
        image_copy(n, 1).start()

    def image_gather(n):
        image_copy(n, 1).wait_recv()

        def add(x, rows):
            R3[x, rows, :] = R1[x, rows, :] + R2[x, rows, :]

        over(n, core, add)
        image_copy(n, 2).start()

    def out_copy(n, h):
        xs, rows = chunk(n, h)
        return pltpu.make_async_copy(R3.at[xs, rows, :], img_out.at[xs, rows, :], osem.at[n, h])

    def image_finish(n):
        if n != 2:
            out_copy(n, core).start()
        image_copy(n, 2).wait_recv()
        if n != 2:
            out_copy(n, 1 - core).start()

    def edge_out(side):
        plane = side * (X - 1)
        return pltpu.make_async_copy(R3.at[plane], img_out.at[plane], osem.at[4, side])

    peers = (dev_c, dev_z, dev_zc)

    def direct(i, side, slot):
        if side is None:
            return pltpu.make_async_remote_copy(
                src_ref=line.at[slot], dst_ref=line.at[slot], send_sem=dsem.at[0, i, 2], recv_sem=dsem.at[1, slot, 2],
                device_id=peers[i], device_id_type=MESH)
        return pltpu.make_async_remote_copy(
            src_ref=D.at[slot, side], dst_ref=D.at[slot, side], send_sem=dsem.at[0, i, side], recv_sem=dsem.at[1, slot, side],
            device_id=peers[i], device_id_type=MESH)

    last = ITERS - 1
    for t in range(ITERS):
        if t == 1:
            interior(0)
        if t == last:
            image_chips(0)
            rest_part(t)
            image_copy(1, 0).start()
            image_copy(3, 0).start()
            y_edge(t, ahead=True)
            image_copy(2, 0).start()
            image_chips(1)
            image_chips(3)
            image_chips(2)
        elif t > 0:
            interior(t)
        if t == last - 1:
            core_part(last)
            image_copy(0, 0).start()
        receive_y(t)
        y_edge(t)
        if t < last:
            send_y(t + 1)
        else:
            line[shot] = corr[:, y_line, :]
            for i in (1, 2, 0):
                direct(i, None, shot).start()
        for side in sides:
            receive_x(t, side)
            if t > 0:
                sent(t - 1, side)
            x_edge(t, side)
            if t < last:
                send_corner(t + 1, side)
                send_x(t + 1, side)
            else:
                for i in (1, 2, 0):
                    direct(i, side, shot).start()
    wave_copy = pltpu.make_async_copy(U.at[ITERS % 2, :, pl.ds(1, X), pl.ds(PAD, Y), :], wave_out.at[0], osem.at[5, 0])
    wave_copy.start()
    order = (0, 1, 3, 2)
    for n in order:
        image_gather(n)
    for n in order:
        image_finish(n)
        for phase in range(3):
            image_copy(n, phase).wait_send()
    slots = (core_pair, z_pair, lax.rem(core_pair + 2, 4))
    for i, slot in enumerate(slots):
        direct(i, None, slot).wait_recv()
    R3[:, y_line, :] = (line[0] + line[1]) + (line[2] + line[3])
    for h in range(2):
        out_copy(2, h).start()
    for side in sides:
        for i, slot in enumerate(slots):
            direct(i, side, slot).wait_recv()
        for j in range(T):
            rows = pl.ds(8 * j, 8)
            total = (D[0, side, rows, :] + D[1, side, rows, :]) + (D[2, side, rows, :] + D[3, side, rows, :])
            R3[side * (X - 1), rows, :] = total
        edge_out(side).start()
    for side in sides:
        sent(last, side)
        for t in range(1, ITERS):
            y_end_copy(t, side).wait_send()
    for side in (*sides, None):
        for i in range(3):
            direct(i, side, shot).wait_send()
    for t in range(ITERS):
        y_copy(t).wait_send()
    for n in range(NC):
        for h in range(2):
            out_copy(n, h).wait()
    for side in sides:
        edge_out(side).wait()
    wave_copy.wait()


def hand_over(wave, image, wave_out, image_out, wave_buf, image_buf, sem):
    half = wave.shape[2] // 2
    parts = []
    for f in range(F):
        for h in range(2):
            xs = pl.ds(h * half, half)
            parts.append((wave.at[0, f, xs], wave_buf.at[f, xs], wave_out.at[0, f, xs]))
    parts.append((image, image_buf, image_out))
    reads = [pltpu.make_async_copy(src, buf, sem.at[0, n]) for n, (src, buf, _) in enumerate(parts)]
    writes = [pltpu.make_async_copy(buf, dst, sem.at[1, n]) for n, (_, buf, dst) in enumerate(parts)]
    for copy in reads:
        copy.start()
    for read, write in zip(reads, writes):
        read.wait()
        write.start()
    for copy in writes:
        copy.wait()


def solution(mesh):
    ngx = mesh.shape["gx"]

    def local(now, prev, vel, eps, dlt, tilt, azim, aper):
        X, Y, Z = vel.shape
        hbm, vm = pl.BlockSpec(memory_space=pltpu.HBM), pltpu.VMEM
        f32 = jnp.float32
        wave, image = pl.pallas_call(
            functools.partial(kernel, (ngx, X, Y, Z)),
            out_shape=(jax.ShapeDtypeStruct(now.shape, f32), jax.ShapeDtypeStruct(vel.shape, f32)),
            in_specs=[hbm] * 7 + [pl.BlockSpec(memory_space=pltpu.SMEM)],
            out_specs=(hbm, hbm),
            scratch_shapes=[
                vm((2, F, X + 2, Y + 2 * PAD, Z), f32),
                vm((3, X, Y, Z), f32),
                vm((2, X, Y, Z), jnp.int32),
                vm((NK, X, Y, Z), f32),
                vm((X, Y, Z), f32),
                vm((X, 8, Z), f32),
                vm((ITERS, F, X, Z), f32),
                vm((ITERS, F, X, Z), f32),
                vm((ITERS, 2, F, Z), f32),
                vm((ITERS, 2, F, Z), f32),
                vm((ITERS, 2, F, Z), f32),
                vm((X, Y, Z), f32),
                vm((X, Y, Z), f32),
                vm((X, Y, Z), f32),
                vm((4, 2, Y, Z), f32),
                vm((4, X, Z), f32),
                pltpu.SemaphoreType.DMA((7,)),
                pltpu.SemaphoreType.DMA((ITERS, 7)),
                pltpu.SemaphoreType.DMA((ITERS, 7)),
                pltpu.SemaphoreType.DMA((2, 3, 4)),
                pltpu.SemaphoreType.DMA((2, 4, 3)),
                pltpu.SemaphoreType.DMA((6, 2)),
            ],
            compiler_params=pltpu.CompilerParams(
                collective_id=0, has_side_effects=True, vmem_limit_bytes=58 * 1024 * 1024),
        )(now, prev, vel, eps, dlt, tilt, azim, aper)
        return pl.pallas_call(
            hand_over,
            out_shape=(jax.ShapeDtypeStruct(now.shape, f32), jax.ShapeDtypeStruct(vel.shape, f32)),
            in_specs=[hbm] * 2,
            out_specs=(hbm, hbm),
            scratch_shapes=[vm(now.shape[1:], f32), vm(vel.shape, f32), pltpu.SemaphoreType.DMA((2, 2 * F + 1))],
            compiler_params=pltpu.CompilerParams(vmem_limit_bytes=58 * 1024 * 1024),
        )(wave, image)

    return jax.shard_map(
        local,
        mesh=mesh,
        in_specs=(
            P("shot", None, "gx", "gy", None),
            P("shot", None, "gx", "gy", None),
            P("gx", "gy", None),
            P("gx", "gy", None),
            P("gx", "gy", None),
            P("gx", "gy", None),
            P("gx", "gy", None),
            P("shot", "gx", "gy"),
        ),
        out_specs=(P("shot", None, "gx", "gy", None), P("gx", "gy", None)),
        check_vma=False,
    )
```

```python
import functools
import math

import jax
import jax.numpy as jnp
from jax import lax
from jax.experimental import pallas as pl
from jax.experimental.pallas import tpu as pltpu
from jax.sharding import PartitionSpec as P

ITERS = 4
F = 4
PAD = 8
MESH = pl.DeviceIdType.MESH
NK = 12
AXX, AYY, BXY, AP, AM, BP, BM, CP, CM, CG, CR, CV = range(NK)


def sin_poly(x, x2):
    return x * (1.0 + x2 * (-1.0 / 6 + x2 * (1.0 / 120 + x2 * (-1.0 / 5040 + x2 * (1.0 / 362880 + x2 * (-1.0 / 39916800 + x2 * (1.0 / 6227020800)))))))


def cos_poly(x2):
    return 1.0 + x2 * (-0.5 + x2 * (1.0 / 24 + x2 * (-1.0 / 720 + x2 * (1.0 / 40320 + x2 * (-1.0 / 3628800 + x2 * (1.0 / 479001600 - x2 * (1.0 / 87178291200)))))))


def normals(tilt, azimuth):
    theta = tilt.astype(jnp.float32) * (math.pi / 180.0)
    t2 = theta * theta
    sin_t, cos_t = sin_poly(theta, t2), cos_poly(t2)
    h = (azimuth - 180).astype(jnp.float32) * (math.pi / 360.0)
    h2 = h * h
    s, c = sin_poly(h, h2), cos_poly(h2)
    s2 = s + s
    return sin_t * (s2 * s - 1.0), -(sin_t * (s2 * c)), cos_t


def kernel(sizes, now, prev, vel, eps, dlt, tilt, azim, aper, wave_out, img_out,
           U, M, A, K, corr, early, P_, Q, PC, QC, QY, R1, R2, R3, D, line, local, ssem, rsem, isem, dsem, osem):
    ngx, X, Y, Z = sizes
    T = Y // 8
    shot, gx, gy = lax.axis_index("shot"), lax.axis_index("gx"), lax.axis_index("gy")
    has_l, has_r = gx > 0, gx < ngx - 1
    core = lax.rem(shot, 2)
    core_pair = shot + 1 - 2 * core
    z_pair = lax.rem(shot + 2, 4)
    other = 1 - gy
    dev_y = (shot, gx, other)
    dev_c, dev_z = (core_pair, gx, gy), (z_pair, gx, gy)
    dev_zc = (lax.rem(core_pair + 2, 4), gx, gy)
    first_side = (lax.rem(gx, 4) == 0).astype(jnp.int32)
    sides = (first_side, 1 - first_side)

    def has(side):
        return jnp.logical_or(jnp.logical_and(side == 0, has_l), jnp.logical_and(side == 1, has_r))
    y_send = PAD + (Y - 1) * (1 - gy)
    y_recv = PAD - 1 + (Y + 1) * (1 - gy)

    loads = []
    for i, ref in enumerate((tilt, azim)):
        loads.append(pltpu.make_async_copy(ref, A.at[i], local.at[i]))
    for i, ref in enumerate((vel, eps, dlt)):
        loads.append(pltpu.make_async_copy(ref, M.at[i], local.at[2 + i]))
    for i, ref in enumerate((now, prev)):
        loads.append(pltpu.make_async_copy(ref.at[0], U.at[i, :, pl.ds(1, X), pl.ds(PAD, Y), :], local.at[5 + i]))
    for copy in loads:
        copy.start()

    barrier = pltpu.get_barrier_semaphore()

    def hello(dev):
        pl.semaphore_signal(barrier, inc=1, device_id=dev, device_id_type=MESH)

    for dev in (dev_y, dev_c, dev_z, dev_zc):
        hello(dev)

    @pl.when(has_l)
    def _():
        hello((shot, gx - 1, gy))
        hello((shot, gx - 1, other))

    @pl.when(has_r)
    def _():
        hello((shot, gx + 1, gy))
        hello((shot, gx + 1, other))

    zero_tile = jnp.zeros((8, Z), jnp.float32)

    def zero_rows(x, c):
        for par in range(2):
            for f in range(F):
                U[par, f, x, pl.ds(0, 8), :] = zero_tile
                U[par, f, x, pl.ds(PAD + Y, 8), :] = zero_tile
        return c

    lax.fori_loop(0, X + 2, zero_rows, 0)

    def zero_plane(x):
        for par in range(2):
            for f in range(F):
                for j in range(T):
                    U[par, f, x, pl.ds(PAD + 8 * j, 8), :] = zero_tile

    @pl.when(jnp.logical_not(has_l))
    def _():
        zero_plane(0)

    @pl.when(jnp.logical_not(has_r))
    def _():
        zero_plane(X + 1)

    pl.semaphore_wait(barrier, 4 + 2 * has_l.astype(jnp.int32) + 2 * has_r.astype(jnp.int32))

    def x_copy(t, side):
        plane = 1 + side * (X - 1)
        return pltpu.make_async_remote_copy(
            src_ref=now.at[0, :, plane - 1] if t == 0 else U.at[t % 2, :, plane, pl.ds(PAD, Y), :],
            dst_ref=U.at[t % 2, :, (1 - side) * (X + 1), pl.ds(PAD, Y), :],
            send_sem=ssem.at[t, side], recv_sem=rsem.at[t, 1 - side],
            device_id=(shot, gx + 2 * side - 1, gy), device_id_type=MESH)

    y_line = (Y - 1) * (1 - gy)

    def corner_copy(t, side):
        return pltpu.make_async_remote_copy(
            src_ref=now.at[0, :, side * (X - 1), y_line, :] if t == 0 else PC.at[t, side], dst_ref=QC.at[t, 1 - side],
            send_sem=ssem.at[t, 3 + side], recv_sem=rsem.at[t, 4 - side],
            device_id=(shot, gx + 2 * side - 1, other), device_id_type=MESH)

    def y_copy(t):
        return pltpu.make_async_remote_copy(
            src_ref=now.at[0, :, :, y_line, :] if t == 0 else P_.at[t], dst_ref=Q.at[t],
            send_sem=ssem.at[t, 2], recv_sem=rsem.at[t, 2], device_id=dev_y, device_id_type=MESH)

    def y_end_copy(t, side):
        return pltpu.make_async_remote_copy(
            src_ref=PC.at[t, side], dst_ref=QY.at[t, side], send_sem=ssem.at[t, 5 + side], recv_sem=rsem.at[t, 5 + side],
            device_id=dev_y, device_id_type=MESH)

    def send_x(t, side):
        @pl.when(has(side))
        def _():
            x_copy(t, side).start()

    def send_corner(t, side):
        if t > 0:
            for f in range(F):
                PC[t, side, pl.ds(f, 1), :] = U[t % 2, f, 1 + side * (X - 1), pl.ds(y_send, 1), :]
            y_end_copy(t, side).start()

        @pl.when(has(side))
        def _():
            corner_copy(t, side).start()

    def send_y(t):
        if t > 0:
            for f in range(F):
                P_[t, f] = U[t % 2, f, pl.ds(1, X), y_send, :]
        y_copy(t).start()

    def receive_y(t):
        y_copy(t).wait_recv()
        for f in range(F):
            U[t % 2, f, pl.ds(1, X), y_recv, :] = Q[t, f]
        if t > 0:
            for side in range(2):
                y_end_copy(t, side).wait_recv()
                for f in range(F):
                    U[t % 2, f, 1 + side * (X - 1), pl.ds(y_recv, 1), :] = QY[t, side, pl.ds(f, 1), :]

    def receive_x(t, side):
        @pl.when(has(side))
        def _():
            x_copy(t, 1 - side).wait_recv()

    def receive_corner(t, side):
        @pl.when(has(side))
        def _():
            corner_copy(t, 1 - side).wait_recv()
            for f in range(F):
                U[t % 2, f, side * (X + 1), pl.ds(y_recv, 1), :] = QC[t, side, pl.ds(f, 1), :]

    def sent(t, side):
        @pl.when(has(side))
        def _():
            x_copy(t, side).wait_send()
            corner_copy(t, side).wait_send()

    send_y(0)
    for side in sides:
        send_corner(0, side)
        send_x(0, side)

    lane = lax.broadcasted_iota(jnp.int32, (8, Z), 1)
    mask_p = jnp.where(lane == 0, 0.0, 1.0)
    mask_m = jnp.where(lane == Z - 1, 0.0, 1.0)
    for i in range(5):
        loads[i].wait()

    def model(i, c):
        for n in range(4 * T):
            x, rows = 4 * i + n // T, pl.ds(8 * (n % T), 8)
            n_x, n_y, n_z = normals(A[0, x, rows, :], A[1, x, rows, :])
            v = M[0, x, rows, :]
            gain = 1.0 + 2.0 * M[1, x, rows, :]
            root = jnp.sqrt(1.0 + 2.0 * M[2, x, rows, :])
            half = 0.5 * n_z
            zz, xz, yz = n_z * n_z, half * n_x, half * n_y
            K[AXX, x, rows, :] = n_x * n_x
            K[AYY, x, rows, :] = n_y * n_y
            K[BXY, x, rows, :] = 0.5 * n_x * n_y
            for value, plus, minus in ((zz, AP, AM), (xz, BP, BM), (yz, CP, CM)):
                K[plus, x, rows, :] = pltpu.roll(value, 1, 1) * mask_p
                K[minus, x, rows, :] = pltpu.roll(value, Z - 1, 1) * mask_m
            K[CG, x, rows, :] = v * gain
            K[CR, x, rows, :] = v * root
            K[CV, x, rows, :] = v
        return c

    lax.fori_loop(0, X // 4, model, 0)
    loads[5].wait()
    loads[6].wait()
    covered = aper[0, 0, 0].astype(jnp.float32) * (1.0 / ITERS)

    edge_row = PAD + (Y - 8) * (1 - gy)
    inner_row = PAD + 8 * gy

    def group(t, x, row, edge=None, ahead=False):
        a, b = t % 2, 1 - t % 2
        row = pl.multiple_of(row, 8)
        here, rows = pl.ds(row, 8), pl.ds(pl.multiple_of(row - PAD, 8), 8)
        k = [K[i, x - 1, rows, :] for i in range(NK)]
        cxx, cyy = 1.0 - k[AXX], 1.0 - k[AYY]
        cap, cam = mask_p - k[AP], mask_m - k[AM]
        centre, op, fresh = [], [], []
        for f in range(F):
            def at(off_x, off_y):
                return U[a, f, x + off_x, pl.ds(row + off_y, 8), :]

            m0, m1, m2 = at(-1, 0), at(0, 0), at(1, 0)
            up, down = at(0, 1), at(0, -1)
            dy, ys = up - down, up + down
            dx, xs = m2 - m0, m2 + m0
            dxy = (at(1, 1) - at(1, -1)) - (at(-1, 1) - at(-1, -1))
            tp = k[BP] * dx + k[CP] * dy
            tm = k[BM] * dx + k[CM] * dy
            mix = k[BXY] * dxy
            if f % 2 == 0:
                sp, sm = cap * m1 - tp, cam * m1 + tm
                side = cxx * xs + cyy * ys - mix
            else:
                sp, sm = k[AP] * m1 + tp, k[AM] * m1 - tm
                side = k[AXX] * xs + k[AYY] * ys + mix
            op.append(side + (pltpu.roll(sp, Z - 1, 1) + pltpu.roll(sm, 1, 1)))
            centre.append(m1)
        for pair in range(F // 2):
            fp, fq = 2 * pair, 2 * pair + 1
            p, q = centre[fp], centre[fq]
            p2, q2 = p + p, q + q
            across, along = op[fp] - (p2 + p2), op[fq] - q2
            p_new = (p2 - U[b, fp, x, here, :]) + (k[CG] * across + k[CR] * along)
            q_new = (q2 - U[b, fq, x, here, :]) + (k[CR] * across + k[CV] * along)
            if not ahead:
                U[b, fp, x, here, :] = p_new
                U[b, fq, x, here, :] = q_new
            fresh.append(p_new)
        prod = fresh[0] * fresh[1]
        if t > 0:
            prod = prod + corr[x - 1, rows, :]
        if t == ITERS - 1:
            prod = prod * covered
        if t == ITERS - 1 and edge is not None:
            D[shot, edge, rows, :] = prod
        elif ahead:
            early[x - 1] = prod
        else:
            corr[x - 1, rows, :] = prod

    far_row = PAD + 16 * gy
    near_row = PAD + Y - 16 - (Y - 24) * gy

    def interior(t):
        def body(i, c):
            for u in range(3):
                for k in range(T - 1):
                    group(t, 2 + 3 * i + u, inner_row + 8 * k)
            return c

        lax.fori_loop(0, (X - 2) // 3, body, 0)

    def core_part(t):
        def body(i, c):
            for u in range(4):
                for k in range(T - 2):
                    group(t, 3 + 4 * i + u, far_row + 8 * k)
            return c

        lax.fori_loop(0, (X - 4) // 4, body, 0)

    def rest_part(t):
        for x in (2, X - 1):
            for k in range(T - 2):
                group(t, x, far_row + 8 * k)

        def body(i, c):
            for u in range(10):
                group(t, 2 + 10 * i + u, near_row)
            return c

        lax.fori_loop(0, (X - 2) // 10, body, 0)

    def y_edge(t, ahead=False):
        def body(i, c):
            for u in range(10):
                group(t, 2 + 10 * i + u, edge_row, ahead=ahead)
            return c

        lax.fori_loop(0, (X - 2) // 10, body, 0)

    def x_edge(t, side):
        plane = 1 + side * (X - 1)
        receive_corner(t, side)
        for j in range(T):
            group(t, plane, PAD + 8 * j, side)

    far = pl.ds(pl.multiple_of(16 * gy, 8), 8 * (T - 2))
    near = pl.ds(pl.multiple_of(Y - 16 - (Y - 24) * gy, 8), 8)
    edge_rows = pl.ds(pl.multiple_of((Y - 8) * (1 - gy), 8), 8)
    CHUNKS = ((2, (X - 4) // 2, (X - 4) // 2, far), (1, X // 2 - 1, X // 2 - 1, near), (1, X // 2 - 1, X // 2 - 1, edge_rows), (1, X - 3, 1, far))
    NC = len(CHUNKS)

    def chunk(n, h):
        low, hop, count, rows = CHUNKS[n]
        return pl.ds(low + h * hop, count), rows

    def image_copy(n, phase):
        mine, theirs = chunk(n, core), chunk(n, 1 - core)

        def make(src, dst, dev):
            return pltpu.make_async_remote_copy(
                src_ref=src, dst_ref=dst, send_sem=isem.at[0, phase, n], recv_sem=isem.at[1, phase, n],
                device_id=dev, device_id_type=MESH)

        if phase == 0:
            return make(early.at[theirs[0]] if n == 2 else corr.at[theirs], R1.at[theirs], dev_c)
        if phase == 1:
            return make(R1.at[mine], R2.at[mine], dev_z)
        return make(R3.at[mine], R3.at[mine], dev_c)

    def over(n, h, fn):
        xs, rows = chunk(n, h)

        def body(i, c):
            for j in range(rows.size // 8):
                fn(xs.start + i, pl.ds(pl.multiple_of(rows.start + 8 * j, 8), 8))
            return c

        if xs.size == 1:
            body(0, 0)
        else:
            lax.fori_loop(0, xs.size, body, 0)

    def image_chips(n):
        image_copy(n, 0).wait_recv()

        def add(x, rows):
            R1[x, rows, :] = R1[x, rows, :] + (early[x] if n == 2 else corr[x, rows, :])

        over(n, core, add)
        image_copy(n, 1).start()

    def image_gather(n):
        image_copy(n, 1).wait_recv()

        def add(x, rows):
            R3[x, rows, :] = R1[x, rows, :] + R2[x, rows, :]

        over(n, core, add)
        image_copy(n, 2).start()

    def out_copy(n, h):
        xs, rows = chunk(n, h)
        return pltpu.make_async_copy(R3.at[xs, rows, :], img_out.at[xs, rows, :], osem.at[n, h])

    def image_finish(n):
        if n != 2:
            out_copy(n, core).start()
        image_copy(n, 2).wait_recv()
        if n != 2:
            out_copy(n, 1 - core).start()

    def edge_out(side):
        plane = side * (X - 1)
        return pltpu.make_async_copy(R3.at[plane], img_out.at[plane], osem.at[4, side])

    peers = (dev_c, dev_z, dev_zc)

    def direct(i, side, slot):
        if side is None:
            return pltpu.make_async_remote_copy(
                src_ref=line.at[slot], dst_ref=line.at[slot], send_sem=dsem.at[0, i, 2], recv_sem=dsem.at[1, slot, 2],
                device_id=peers[i], device_id_type=MESH)
        return pltpu.make_async_remote_copy(
            src_ref=D.at[slot, side], dst_ref=D.at[slot, side], send_sem=dsem.at[0, i, side], recv_sem=dsem.at[1, slot, side],
            device_id=peers[i], device_id_type=MESH)

    last = ITERS - 1
    for t in range(ITERS):
        if t == 1:
            interior(0)
        if t == last:
            image_chips(0)
            rest_part(t)
            image_copy(1, 0).start()
            image_copy(3, 0).start()
            y_edge(t, ahead=True)
            image_copy(2, 0).start()
            image_chips(1)
            image_chips(3)
            image_chips(2)
        elif t > 0:
            interior(t)
        if t == last - 1:
            core_part(last)
            image_copy(0, 0).start()
        receive_y(t)
        y_edge(t)
        if t < last:
            send_y(t + 1)
        else:
            line[shot] = corr[:, y_line, :]
            for i in (1, 2, 0):
                direct(i, None, shot).start()
        for side in sides:
            receive_x(t, side)
            if t > 0:
                sent(t - 1, side)
            x_edge(t, side)
            if t < last:
                send_corner(t + 1, side)
                send_x(t + 1, side)
            else:
                for i in (1, 2, 0):
                    direct(i, side, shot).start()
    wave_copy = pltpu.make_async_copy(U.at[ITERS % 2, :, pl.ds(1, X), pl.ds(PAD, Y), :], wave_out.at[0], osem.at[5, 0])
    wave_copy.start()
    order = (0, 1, 3, 2)
    for n in order:
        image_gather(n)
    for n in order:
        image_finish(n)
        for phase in range(3):
            image_copy(n, phase).wait_send()
    slots = (core_pair, z_pair, lax.rem(core_pair + 2, 4))
    for i, slot in enumerate(slots):
        direct(i, None, slot).wait_recv()
    R3[:, y_line, :] = (line[0] + line[1]) + (line[2] + line[3])
    for h in range(2):
        out_copy(2, h).start()
    for side in sides:
        for i, slot in enumerate(slots):
            direct(i, side, slot).wait_recv()
        for j in range(T):
            rows = pl.ds(8 * j, 8)
            total = (D[0, side, rows, :] + D[1, side, rows, :]) + (D[2, side, rows, :] + D[3, side, rows, :])
            R3[side * (X - 1), rows, :] = total
        edge_out(side).start()
    for side in sides:
        sent(last, side)
        for t in range(1, ITERS):
            y_end_copy(t, side).wait_send()
    for side in (*sides, None):
        for i in range(3):
            direct(i, side, shot).wait_send()
    for t in range(ITERS):
        y_copy(t).wait_send()
    for n in range(NC):
        for h in range(2):
            out_copy(n, h).wait()
    for side in sides:
        edge_out(side).wait()
    wave_copy.wait()


def hand_over(wave, image, wave_out, image_out, wave_buf, image_buf, sem):
    half = wave.shape[2] // 2
    parts = []
    for f in range(F):
        for h in range(2):
            xs = pl.ds(h * half, half)
            parts.append((wave.at[0, f, xs], wave_buf.at[f, xs], wave_out.at[0, f, xs]))
    parts.append((image, image_buf, image_out))
    reads = [pltpu.make_async_copy(src, buf, sem.at[0, n]) for n, (src, buf, _) in enumerate(parts)]
    writes = [pltpu.make_async_copy(buf, dst, sem.at[1, n]) for n, (_, buf, dst) in enumerate(parts)]
    for copy in reads:
        copy.start()
    for read, write in zip(reads, writes):
        read.wait()
        write.start()
    for copy in writes:
        copy.wait()


def solution(mesh):
    ngx = mesh.shape["gx"]

    def local(now, prev, vel, eps, dlt, tilt, azim, aper):
        X, Y, Z = vel.shape
        hbm, vm = pl.BlockSpec(memory_space=pltpu.HBM), pltpu.VMEM
        f32 = jnp.float32
        wave, image = pl.pallas_call(
            functools.partial(kernel, (ngx, X, Y, Z)),
            out_shape=(jax.ShapeDtypeStruct(now.shape, f32), jax.ShapeDtypeStruct(vel.shape, f32)),
            in_specs=[hbm] * 7 + [pl.BlockSpec(memory_space=pltpu.SMEM)],
            out_specs=(hbm, hbm),
            scratch_shapes=[
                vm((2, F, X + 2, Y + 2 * PAD, Z), f32),
                vm((3, X, Y, Z), f32),
                vm((2, X, Y, Z), jnp.int32),
                vm((NK, X, Y, Z), f32),
                vm((X, Y, Z), f32),
                vm((X, 8, Z), f32),
                vm((ITERS, F, X, Z), f32),
                vm((ITERS, F, X, Z), f32),
                vm((ITERS, 2, F, Z), f32),
                vm((ITERS, 2, F, Z), f32),
                vm((ITERS, 2, F, Z), f32),
                vm((X, Y, Z), f32),
                vm((X, Y, Z), f32),
                vm((X, Y, Z), f32),
                vm((4, 2, Y, Z), f32),
                vm((4, X, Z), f32),
                pltpu.SemaphoreType.DMA((7,)),
                pltpu.SemaphoreType.DMA((ITERS, 7)),
                pltpu.SemaphoreType.DMA((ITERS, 7)),
                pltpu.SemaphoreType.DMA((2, 3, 4)),
                pltpu.SemaphoreType.DMA((2, 4, 3)),
                pltpu.SemaphoreType.DMA((6, 2)),
            ],
            compiler_params=pltpu.CompilerParams(
                collective_id=0, has_side_effects=True, vmem_limit_bytes=58 * 1024 * 1024),
        )(now, prev, vel, eps, dlt, tilt, azim, aper)
        return pl.pallas_call(
            hand_over,
            out_shape=(jax.ShapeDtypeStruct(now.shape, f32), jax.ShapeDtypeStruct(vel.shape, f32)),
            in_specs=[hbm] * 2,
            out_specs=(hbm, hbm),
            scratch_shapes=[vm(now.shape[1:], f32), vm(vel.shape, f32), pltpu.SemaphoreType.DMA((2, 2 * F + 1))],
            compiler_params=pltpu.CompilerParams(vmem_limit_bytes=58 * 1024 * 1024),
        )(wave, image)

    return jax.shard_map(
        local,
        mesh=mesh,
        in_specs=(
            P("shot", None, "gx", "gy", None),
            P("shot", None, "gx", "gy", None),
            P("gx", "gy", None),
            P("gx", "gy", None),
            P("gx", "gy", None),
            P("gx", "gy", None),
            P("gx", "gy", None),
            P("shot", "gx", "gy"),
        ),
        out_specs=(P("shot", None, "gx", "gy", None), P("gx", "gy", None)),
        check_vma=False,
    )
```

```python
import functools
import math

import jax
import jax.numpy as jnp
from jax import lax
from jax.experimental import pallas as pl
from jax.experimental.pallas import tpu as pltpu
from jax.sharding import PartitionSpec as P

ITERS = 4
F = 4
PAD = 8
MESH = pl.DeviceIdType.MESH
NK = 12
AXX, AYY, BXY, AP, AM, BP, BM, CP, CM, CG, CR, CV = range(NK)


def sin_poly(x, x2):
    return x * (1.0 + x2 * (-1.0 / 6 + x2 * (1.0 / 120 + x2 * (-1.0 / 5040 + x2 * (1.0 / 362880 + x2 * (-1.0 / 39916800 + x2 * (1.0 / 6227020800)))))))


def cos_poly(x2):
    return 1.0 + x2 * (-0.5 + x2 * (1.0 / 24 + x2 * (-1.0 / 720 + x2 * (1.0 / 40320 + x2 * (-1.0 / 3628800 + x2 * (1.0 / 479001600 - x2 * (1.0 / 87178291200)))))))


def normals(tilt, azimuth):
    theta = tilt.astype(jnp.float32) * (math.pi / 180.0)
    t2 = theta * theta
    sin_t, cos_t = sin_poly(theta, t2), cos_poly(t2)
    h = (azimuth - 180).astype(jnp.float32) * (math.pi / 360.0)
    h2 = h * h
    s, c = sin_poly(h, h2), cos_poly(h2)
    s2 = s + s
    return sin_t * (s2 * s - 1.0), -(sin_t * (s2 * c)), cos_t


def kernel(sizes, now, prev, vel, eps, dlt, tilt, azim, aper, wave_out, img_out,
           U, M, A, K, corr, early, P_, Q, PC, QC, QY, R1, R2, R3, D, line, local, ssem, rsem, isem, dsem, osem):
    ngx, X, Y, Z = sizes
    T = Y // 8
    shot, gx, gy = lax.axis_index("shot"), lax.axis_index("gx"), lax.axis_index("gy")
    has_l, has_r = gx > 0, gx < ngx - 1
    core = lax.rem(shot, 2)
    core_pair = shot + 1 - 2 * core
    z_pair = lax.rem(shot + 2, 4)
    other = 1 - gy
    dev_y = (shot, gx, other)
    dev_c, dev_z = (core_pair, gx, gy), (z_pair, gx, gy)
    dev_zc = (lax.rem(core_pair + 2, 4), gx, gy)
    first_side = (lax.rem(gx, 4) == 0).astype(jnp.int32)
    sides = (first_side, 1 - first_side)

    def has(side):
        return jnp.logical_or(jnp.logical_and(side == 0, has_l), jnp.logical_and(side == 1, has_r))
    y_send = PAD + (Y - 1) * (1 - gy)
    y_recv = PAD - 1 + (Y + 1) * (1 - gy)

    loads = []
    for i, ref in enumerate((tilt, azim)):
        loads.append(pltpu.make_async_copy(ref, A.at[i], local.at[i]))
    for i, ref in enumerate((vel, eps, dlt)):
        loads.append(pltpu.make_async_copy(ref, M.at[i], local.at[2 + i]))
    for i, ref in enumerate((now, prev)):
        loads.append(pltpu.make_async_copy(ref.at[0], U.at[i, :, pl.ds(1, X), pl.ds(PAD, Y), :], local.at[5 + i]))
    for copy in loads:
        copy.start()

    barrier = pltpu.get_barrier_semaphore()

    def hello(dev):
        pl.semaphore_signal(barrier, inc=1, device_id=dev, device_id_type=MESH)

    for dev in (dev_y, dev_c, dev_z, dev_zc):
        hello(dev)

    @pl.when(has_l)
    def _():
        hello((shot, gx - 1, gy))
        hello((shot, gx - 1, other))

    @pl.when(has_r)
    def _():
        hello((shot, gx + 1, gy))
        hello((shot, gx + 1, other))

    zero_tile = jnp.zeros((8, Z), jnp.float32)

    def zero_rows(x, c):
        for par in range(2):
            for f in range(F):
                U[par, f, x, pl.ds(0, 8), :] = zero_tile
                U[par, f, x, pl.ds(PAD + Y, 8), :] = zero_tile
        return c

    lax.fori_loop(0, X + 2, zero_rows, 0)

    def zero_plane(x):
        for par in range(2):
            for f in range(F):
                for j in range(T):
                    U[par, f, x, pl.ds(PAD + 8 * j, 8), :] = zero_tile

    @pl.when(jnp.logical_not(has_l))
    def _():
        zero_plane(0)

    @pl.when(jnp.logical_not(has_r))
    def _():
        zero_plane(X + 1)

    pl.semaphore_wait(barrier, 4 + 2 * has_l.astype(jnp.int32) + 2 * has_r.astype(jnp.int32))

    def x_copy(t, side):
        plane = 1 + side * (X - 1)
        return pltpu.make_async_remote_copy(
            src_ref=now.at[0, :, plane - 1] if t == 0 else U.at[t % 2, :, plane, pl.ds(PAD, Y), :],
            dst_ref=U.at[t % 2, :, (1 - side) * (X + 1), pl.ds(PAD, Y), :],
            send_sem=ssem.at[t, side], recv_sem=rsem.at[t, 1 - side],
            device_id=(shot, gx + 2 * side - 1, gy), device_id_type=MESH)

    y_line = (Y - 1) * (1 - gy)

    def corner_copy(t, side):
        return pltpu.make_async_remote_copy(
            src_ref=now.at[0, :, side * (X - 1), y_line, :] if t == 0 else PC.at[t, side], dst_ref=QC.at[t, 1 - side],
            send_sem=ssem.at[t, 3 + side], recv_sem=rsem.at[t, 4 - side],
            device_id=(shot, gx + 2 * side - 1, other), device_id_type=MESH)

    def y_copy(t):
        return pltpu.make_async_remote_copy(
            src_ref=now.at[0, :, :, y_line, :] if t == 0 else P_.at[t], dst_ref=Q.at[t],
            send_sem=ssem.at[t, 2], recv_sem=rsem.at[t, 2], device_id=dev_y, device_id_type=MESH)

    def y_end_copy(t, side):
        return pltpu.make_async_remote_copy(
            src_ref=PC.at[t, side], dst_ref=QY.at[t, side], send_sem=ssem.at[t, 5 + side], recv_sem=rsem.at[t, 5 + side],
            device_id=dev_y, device_id_type=MESH)

    def send_x(t, side):
        @pl.when(has(side))
        def _():
            x_copy(t, side).start()

    def send_corner(t, side):
        if t > 0:
            for f in range(F):
                PC[t, side, pl.ds(f, 1), :] = U[t % 2, f, 1 + side * (X - 1), pl.ds(y_send, 1), :]

        @pl.when(has(side))
        def _():
            corner_copy(t, side).start()

    def send_y(t):
        if t > 0:
            for f in range(F):
                P_[t, f] = U[t % 2, f, pl.ds(1, X), y_send, :]
        y_copy(t).start()

    def receive_y(t):
        y_copy(t).wait_recv()
        for f in range(F):
            U[t % 2, f, pl.ds(1, X), y_recv, :] = Q[t, f]
        if t > 0:
            for side in range(2):
                y_end_copy(t, side).wait_recv()
                for f in range(F):
                    U[t % 2, f, 1 + side * (X - 1), pl.ds(y_recv, 1), :] = QY[t, side, pl.ds(f, 1), :]

    def receive_x(t, side):
        @pl.when(has(side))
        def _():
            x_copy(t, 1 - side).wait_recv()

    def receive_corner(t, side):
        @pl.when(has(side))
        def _():
            corner_copy(t, 1 - side).wait_recv()
            for f in range(F):
                U[t % 2, f, side * (X + 1), pl.ds(y_recv, 1), :] = QC[t, side, pl.ds(f, 1), :]

    def sent(t, side):
        @pl.when(has(side))
        def _():
            x_copy(t, side).wait_send()
            corner_copy(t, side).wait_send()

    send_y(0)
    for side in sides:
        send_corner(0, side)
        send_x(0, side)

    lane = lax.broadcasted_iota(jnp.int32, (8, Z), 1)
    mask_p = jnp.where(lane == 0, 0.0, 1.0)
    mask_m = jnp.where(lane == Z - 1, 0.0, 1.0)
    for i in range(5):
        loads[i].wait()

    def model(i, c):
        for n in range(4 * T):
            x, rows = 4 * i + n // T, pl.ds(8 * (n % T), 8)
            n_x, n_y, n_z = normals(A[0, x, rows, :], A[1, x, rows, :])
            v = M[0, x, rows, :]
            gain = 1.0 + 2.0 * M[1, x, rows, :]
            root = jnp.sqrt(1.0 + 2.0 * M[2, x, rows, :])
            half = 0.5 * n_z
            zz, xz, yz = n_z * n_z, half * n_x, half * n_y
            K[AXX, x, rows, :] = n_x * n_x
            K[AYY, x, rows, :] = n_y * n_y
            K[BXY, x, rows, :] = 0.5 * n_x * n_y
            for value, plus, minus in ((zz, AP, AM), (xz, BP, BM), (yz, CP, CM)):
                K[plus, x, rows, :] = pltpu.roll(value, 1, 1) * mask_p
                K[minus, x, rows, :] = pltpu.roll(value, Z - 1, 1) * mask_m
            K[CG, x, rows, :] = v * gain
            K[CR, x, rows, :] = v * root
            K[CV, x, rows, :] = v
        return c

    lax.fori_loop(0, X // 4, model, 0)
    loads[5].wait()
    loads[6].wait()
    covered = aper[0, 0, 0].astype(jnp.float32) * (1.0 / ITERS)

    edge_row = PAD + (Y - 8) * (1 - gy)
    inner_row = PAD + 8 * gy

    def group(t, x, row, edge=None, ahead=False):
        a, b = t % 2, 1 - t % 2
        row = pl.multiple_of(row, 8)
        here, rows = pl.ds(row, 8), pl.ds(pl.multiple_of(row - PAD, 8), 8)
        k = [K[i, x - 1, rows, :] for i in range(NK)]
        cxx, cyy = 1.0 - k[AXX], 1.0 - k[AYY]
        cap, cam = mask_p - k[AP], mask_m - k[AM]
        centre, op, fresh = [], [], []
        for f in range(F):
            def at(off_x, off_y):
                return U[a, f, x + off_x, pl.ds(row + off_y, 8), :]

            m0, m1, m2 = at(-1, 0), at(0, 0), at(1, 0)
            up, down = at(0, 1), at(0, -1)
            dy, ys = up - down, up + down
            dx, xs = m2 - m0, m2 + m0
            dxy = (at(1, 1) - at(1, -1)) - (at(-1, 1) - at(-1, -1))
            tp = k[BP] * dx + k[CP] * dy
            tm = k[BM] * dx + k[CM] * dy
            mix = k[BXY] * dxy
            if f % 2 == 0:
                sp, sm = cap * m1 - tp, cam * m1 + tm
                side = cxx * xs + cyy * ys - mix
            else:
                sp, sm = k[AP] * m1 + tp, k[AM] * m1 - tm
                side = k[AXX] * xs + k[AYY] * ys + mix
            op.append(side + (pltpu.roll(sp, Z - 1, 1) + pltpu.roll(sm, 1, 1)))
            centre.append(m1)
        for pair in range(F // 2):
            fp, fq = 2 * pair, 2 * pair + 1
            p, q = centre[fp], centre[fq]
            p2, q2 = p + p, q + q
            across, along = op[fp] - (p2 + p2), op[fq] - q2
            p_new = (p2 - U[b, fp, x, here, :]) + (k[CG] * across + k[CR] * along)
            q_new = (q2 - U[b, fq, x, here, :]) + (k[CR] * across + k[CV] * along)
            if not ahead:
                U[b, fp, x, here, :] = p_new
                U[b, fq, x, here, :] = q_new
            fresh.append(p_new)
        prod = fresh[0] * fresh[1]
        if t > 0:
            prod = prod + corr[x - 1, rows, :]
        if t == ITERS - 1:
            prod = prod * covered
        if t == ITERS - 1 and edge is not None:
            D[shot, edge, rows, :] = prod
        elif ahead:
            early[x - 1] = prod
        else:
            corr[x - 1, rows, :] = prod

    far_row = PAD + 16 * gy
    near_row = PAD + Y - 16 - (Y - 24) * gy

    def interior(t):
        def body(i, c):
            for u in range(3):
                for k in range(T - 1):
                    group(t, 2 + 3 * i + u, inner_row + 8 * k)
            return c

        lax.fori_loop(0, (X - 2) // 3, body, 0)

    def core_part(t):
        def body(i, c):
            for u in range(4):
                for k in range(T - 2):
                    group(t, 3 + 4 * i + u, far_row + 8 * k)
            return c

        lax.fori_loop(0, (X - 4) // 4, body, 0)

    def rest_part(t):
        for x in (2, X - 1):
            for k in range(T - 2):
                group(t, x, far_row + 8 * k)

        def body(i, c):
            for u in range(10):
                group(t, 2 + 10 * i + u, near_row)
            return c

        lax.fori_loop(0, (X - 2) // 10, body, 0)

    def y_edge(t, ahead=False):
        def body(i, c):
            for u in range(10):
                group(t, 2 + 10 * i + u, edge_row, ahead=ahead)
            return c

        lax.fori_loop(0, (X - 2) // 10, body, 0)

    def x_edge(t, side):
        plane = 1 + side * (X - 1)
        receive_corner(t, side)
        for j in range(T):
            group(t, plane, PAD + 8 * j, side)

    far = pl.ds(pl.multiple_of(16 * gy, 8), 8 * (T - 2))
    near = pl.ds(pl.multiple_of(Y - 16 - (Y - 24) * gy, 8), 8)
    edge_rows = pl.ds(pl.multiple_of((Y - 8) * (1 - gy), 8), 8)
    CHUNKS = ((2, (X - 4) // 2, (X - 4) // 2, far), (1, X // 2 - 1, X // 2 - 1, near), (1, X // 2 - 1, X // 2 - 1, edge_rows), (1, X - 3, 1, far))
    NC = len(CHUNKS)

    def chunk(n, h):
        low, hop, count, rows = CHUNKS[n]
        return pl.ds(low + h * hop, count), rows

    def image_copy(n, phase):
        mine, theirs = chunk(n, core), chunk(n, 1 - core)

        def make(src, dst, dev):
            return pltpu.make_async_remote_copy(
                src_ref=src, dst_ref=dst, send_sem=isem.at[0, phase, n], recv_sem=isem.at[1, phase, n],
                device_id=dev, device_id_type=MESH)

        if phase == 0:
            return make(early.at[theirs[0]] if n == 2 else corr.at[theirs], R1.at[theirs], dev_c)
        if phase == 1:
            return make(R1.at[mine], R2.at[mine], dev_z)
        return make(R3.at[mine], R3.at[mine], dev_c)

    def over(n, h, fn):
        xs, rows = chunk(n, h)

        def body(i, c):
            for j in range(rows.size // 8):
                fn(xs.start + i, pl.ds(pl.multiple_of(rows.start + 8 * j, 8), 8))
            return c

        if xs.size == 1:
            body(0, 0)
        else:
            lax.fori_loop(0, xs.size, body, 0)

    def image_chips(n):
        image_copy(n, 0).wait_recv()

        def add(x, rows):
            R1[x, rows, :] = R1[x, rows, :] + (early[x] if n == 2 else corr[x, rows, :])

        over(n, core, add)
        image_copy(n, 1).start()

    def image_gather(n):
        image_copy(n, 1).wait_recv()

        def add(x, rows):
            R3[x, rows, :] = R1[x, rows, :] + R2[x, rows, :]

        over(n, core, add)
        image_copy(n, 2).start()

    def out_copy(n, h):
        xs, rows = chunk(n, h)
        return pltpu.make_async_copy(R3.at[xs, rows, :], img_out.at[xs, rows, :], osem.at[n, h])

    def image_finish(n):
        if n != 2:
            out_copy(n, core).start()
        image_copy(n, 2).wait_recv()
        if n != 2:
            out_copy(n, 1 - core).start()

    def edge_out(side):
        plane = side * (X - 1)
        return pltpu.make_async_copy(R3.at[plane], img_out.at[plane], osem.at[4, side])

    peers = (dev_c, dev_z, dev_zc)

    def direct(i, side, slot):
        if side is None:
            return pltpu.make_async_remote_copy(
                src_ref=line.at[slot], dst_ref=line.at[slot], send_sem=dsem.at[0, i, 2], recv_sem=dsem.at[1, slot, 2],
                device_id=peers[i], device_id_type=MESH)
        return pltpu.make_async_remote_copy(
            src_ref=D.at[slot, side], dst_ref=D.at[slot, side], send_sem=dsem.at[0, i, side], recv_sem=dsem.at[1, slot, side],
            device_id=peers[i], device_id_type=MESH)

    last = ITERS - 1
    for t in range(ITERS):
        if t == 1:
            interior(0)
        if t == last:
            image_chips(0)
            rest_part(t)
            image_copy(1, 0).start()
            image_copy(3, 0).start()
            y_edge(t, ahead=True)
            image_copy(2, 0).start()
            image_chips(1)
            image_chips(3)
            image_chips(2)
        elif t > 0:
            interior(t)
        if t == last - 1:
            core_part(last)
            image_copy(0, 0).start()
        receive_y(t)
        y_edge(t)
        if t < last:
            send_y(t + 1)
        else:
            line[shot] = corr[:, y_line, :]
            for i in (1, 2, 0):
                direct(i, None, shot).start()
        for side in sides:
            receive_x(t, side)
            if t > 0:
                sent(t - 1, side)
            x_edge(t, side)
            if t < last:
                send_corner(t + 1, side)
                send_x(t + 1, side)
                y_end_copy(t + 1, side).start()
            else:
                for i in (1, 2, 0):
                    direct(i, side, shot).start()
    wave_copy = pltpu.make_async_copy(U.at[ITERS % 2, :, pl.ds(1, X), pl.ds(PAD, Y), :], wave_out.at[0], osem.at[5, 0])
    wave_copy.start()
    order = (0, 1, 3, 2)
    for n in order:
        image_gather(n)
    for n in order:
        image_finish(n)
        for phase in range(3):
            image_copy(n, phase).wait_send()
    slots = (core_pair, z_pair, lax.rem(core_pair + 2, 4))
    for i, slot in enumerate(slots):
        direct(i, None, slot).wait_recv()
    R3[:, y_line, :] = (line[0] + line[1]) + (line[2] + line[3])
    for h in range(2):
        out_copy(2, h).start()
    for side in sides:
        for i, slot in enumerate(slots):
            direct(i, side, slot).wait_recv()
        for j in range(T):
            rows = pl.ds(8 * j, 8)
            total = (D[0, side, rows, :] + D[1, side, rows, :]) + (D[2, side, rows, :] + D[3, side, rows, :])
            R3[side * (X - 1), rows, :] = total
        edge_out(side).start()
    for side in sides:
        sent(last, side)
        for t in range(1, ITERS):
            y_end_copy(t, side).wait_send()
    for side in (*sides, None):
        for i in range(3):
            direct(i, side, shot).wait_send()
    for t in range(ITERS):
        y_copy(t).wait_send()
    for n in range(NC):
        for h in range(2):
            out_copy(n, h).wait()
    for side in sides:
        edge_out(side).wait()
    wave_copy.wait()


def hand_over(wave, image, wave_out, image_out, wave_buf, image_buf, sem):
    parts = []
    for f in range(F):
        parts.append((wave.at[0, f], wave_buf.at[f], wave_out.at[0, f]))
    parts.append((image, image_buf, image_out))
    reads = [pltpu.make_async_copy(src, buf, sem.at[0, n]) for n, (src, buf, _) in enumerate(parts)]
    writes = [pltpu.make_async_copy(buf, dst, sem.at[1, n]) for n, (_, buf, dst) in enumerate(parts)]
    for copy in reads:
        copy.start()
    for read, write in zip(reads, writes):
        read.wait()
        write.start()
    for copy in writes:
        copy.wait()


def solution(mesh):
    ngx = mesh.shape["gx"]

    def local(now, prev, vel, eps, dlt, tilt, azim, aper):
        X, Y, Z = vel.shape
        hbm, vm = pl.BlockSpec(memory_space=pltpu.HBM), pltpu.VMEM
        f32 = jnp.float32
        wave, image = pl.pallas_call(
            functools.partial(kernel, (ngx, X, Y, Z)),
            out_shape=(jax.ShapeDtypeStruct(now.shape, f32), jax.ShapeDtypeStruct(vel.shape, f32)),
            in_specs=[hbm] * 7 + [pl.BlockSpec(memory_space=pltpu.SMEM)],
            out_specs=(hbm, hbm),
            scratch_shapes=[
                vm((2, F, X + 2, Y + 2 * PAD, Z), f32),
                vm((3, X, Y, Z), f32),
                vm((2, X, Y, Z), jnp.int32),
                vm((NK, X, Y, Z), f32),
                vm((X, Y, Z), f32),
                vm((X, 8, Z), f32),
                vm((ITERS, F, X, Z), f32),
                vm((ITERS, F, X, Z), f32),
                vm((ITERS, 2, F, Z), f32),
                vm((ITERS, 2, F, Z), f32),
                vm((ITERS, 2, F, Z), f32),
                vm((X, Y, Z), f32),
                vm((X, Y, Z), f32),
                vm((X, Y, Z), f32),
                vm((4, 2, Y, Z), f32),
                vm((4, X, Z), f32),
                pltpu.SemaphoreType.DMA((7,)),
                pltpu.SemaphoreType.DMA((ITERS, 7)),
                pltpu.SemaphoreType.DMA((ITERS, 7)),
                pltpu.SemaphoreType.DMA((2, 3, 4)),
                pltpu.SemaphoreType.DMA((2, 4, 3)),
                pltpu.SemaphoreType.DMA((6, 2)),
            ],
            compiler_params=pltpu.CompilerParams(
                collective_id=0, has_side_effects=True, vmem_limit_bytes=58 * 1024 * 1024),
        )(now, prev, vel, eps, dlt, tilt, azim, aper)
        return pl.pallas_call(
            hand_over,
            out_shape=(jax.ShapeDtypeStruct(now.shape, f32), jax.ShapeDtypeStruct(vel.shape, f32)),
            in_specs=[hbm] * 2,
            out_specs=(hbm, hbm),
            scratch_shapes=[vm(now.shape[1:], f32), vm(vel.shape, f32), pltpu.SemaphoreType.DMA((2, F + 1))],
            compiler_params=pltpu.CompilerParams(vmem_limit_bytes=58 * 1024 * 1024),
        )(wave, image)

    return jax.shard_map(
        local,
        mesh=mesh,
        in_specs=(
            P("shot", None, "gx", "gy", None),
            P("shot", None, "gx", "gy", None),
            P("gx", "gy", None),
            P("gx", "gy", None),
            P("gx", "gy", None),
            P("gx", "gy", None),
            P("gx", "gy", None),
            P("shot", "gx", "gy"),
        ),
        out_specs=(P("shot", None, "gx", "gy", None), P("gx", "gy", None)),
        check_vma=False,
    )
```
